128 devices in a mesh: dp: 2 (over core), expert: 64 (over z, y, x).
Axes of the slice: x: 4, y: 4, z: 4, core: 2. Of those that a mesh axis runs over, the one named last changes fastest.
Arguments:
- tokens: bfloat16 [8192, 1792], P(('dp', 'expert')), may hold values from -6 to 6
- grad_out: bfloat16 [8192, 1792], P(('dp', 'expert')), may hold values from -6 to 6
- combine: float32 [8192, 8], P(('dp', 'expert')), may hold values from 0.02 to 0.3
- expert_ids: int32 [8192, 8], P(('dp', 'expert')), may hold values from 0 to 63, all different within a row; in each aligned block of 64 rows (0 to 63, 64 to 127, ...) at most 12 rows name the same one
- w_gate: bfloat16 [64, 1792, 1280], P('expert', 'dp'), may hold values from -0.125 to 0.125
- w_up: bfloat16 [64, 1792, 1280], P('expert', 'dp'), may hold values from -0.125 to 0.125
- w_down: bfloat16 [64, 1792, 1280], P('expert', 'dp'), may hold values from -0.15625 to 0.15625
Outputs:
- token_grad: bfloat16 [8192, 1792], P(('dp', 'expert'))
- grad_w_gate: bfloat16 [64, 1792, 1280], P('expert', 'dp')
- grad_w_up: bfloat16 [64, 1792, 1280], P('expert', 'dp')
- grad_w_down: bfloat16 [64, 1792, 1280], P('expert', 'dp')
The draws below stay inside these ranges and needn't reach their ends.
Inputs may be any that keep to these rules, and one draw needn't show every extreme that they name: `expert_ids`: each row names 8 different experts; within the rows of one device no expert is named more than 12 times.
All inputs are finite; a program needn't handle non-finite values.
Results may differ from the reference program's by a relative error of at most 0.0066.
Values may be sent and summed in bfloat16 or wider, within the bound.
A program may use at most 128 MiB of HBM per device.

```python
import math
import jax
import jax.numpy as jnp
import numpy as np
from jax import lax

D = 1792
FF = 1280
TOP = 8
TOK_DEV = 64
EXPERTS = 64
CAPS = 12
TOKENS = 8192
N_DP = 2
N_EXPERT = 64


def block_levels(stream_key, extent, pieces, smallest, top_value):
    def one(dim, shards_of):
        steps = jax.random.uniform(jax.random.fold_in(jax.random.fold_in(stream_key, 6), dim), (shards_of,), jnp.float32, smallest / len(pieces), top_value / len(pieces))
        return jnp.repeat(jnp.exp(steps), extent[dim] // shards_of).reshape((-1,) + (1,) * (len(extent) - dim - 1))

    factor_of = one(*pieces[0])
    for cut in pieces[1:]:
        factor_of = factor_of * one(*cut)
    return factor_of


def deal_out(own_key, own, number, rows, count, top, reach, slope):
    order = jax.random.permutation(own_key, count)
    heavy_load, common = shares(count, rows * top, reach, slope, True), shares(count, rows * top, reach, slope, False)
    places = jnp.arange(count)

    def named(tallies, rotation):
        used = int((tallies > 0).sum())
        fixed = max(1, used // 4)
        shifted = fixed + (places - fixed + rotation * (used - fixed)) % max(1, count - fixed)
        return jnp.zeros((count,), jnp.int32).at[order[jnp.where(places < fixed, places, shifted)]].set(jnp.asarray(tallies, jnp.int32))

    tallies = jnp.where(number % 4 == 0, named(heavy_load, number // 4), named(common, number - number // 4 - 1))
    mixed = jax.random.permutation(jax.random.fold_in(own, 3), count)
    giver, taker = mixed[0:count // 2 * 2:2], mixed[1:count // 2 * 2:2]
    margin = jnp.minimum(tallies[giver] - 1, reach - tallies[taker]) // 2
    margin = jnp.where((giver == order[0]) | (taker == order[0]) | (tallies[taker] == 0), 0, jnp.maximum(margin, 0))
    shifted = jax.random.randint(jax.random.fold_in(own, 4), (count // 2,), 0, 1 << 20) % (margin + 1)
    tallies = tallies.at[giver].add(-shifted).at[taker].add(shifted)
    members = jnp.searchsorted(jnp.cumsum(tallies), jnp.arange(rows * top), side="right").astype(jnp.int32)
    table = members.reshape(top, rows).T
    table = table[jax.random.permutation(jax.random.fold_in(own, 1), rows)]
    rotation = jax.random.randint(jax.random.fold_in(own, 2), (rows, 1), 0, top)
    return jnp.take_along_axis(table, (jnp.arange(top)[None, :] + rotation) % top, axis=1)


def shares(count, total, limit, lean, full):
    portions = [(1 << 20) // math.isqrt(rank ** lean) + 1 for rank in range(1, count + 1)]
    largest = limit if full else min(limit, max(-(-total // count), total * portions[0] // sum(portions)))
    least = 1 if total - largest >= count - 1 else 0
    counts, rest = [largest] + [least] * (count - 1), total - largest - least * (count - 1)
    while rest > 0:
        movable = [i for i in range(1, count) if counts[i] < largest] or [i for i in range(1, count) if counts[i] < limit]
        whole, left = sum([portions[i] for i in movable]), rest
        for i in movable:
            addition = min(limit - counts[i], max(1, left * portions[i] // whole), rest)
            counts[i] = counts[i] + addition
            rest = rest - addition
    return np.array(counts)


def centred(rng, extent, spread, bound, split=(), kind=jnp.bfloat16):
    result = spread * jax.random.normal(rng, extent, jnp.float32)
    if split:
        result = result * block_levels(rng, extent, split, -0.22, 0.18)
    return jnp.clip(result, -bound, bound).astype(kind)


def setup_inputs(seed: int = 0) -> dict:
    arg_keys = jax.random.split(jax.random.key(seed), 8)
    tokens = centred(arg_keys[0], (TOKENS, D), 1.0, 6.0, ((0, 128),))
    grad_out = centred(arg_keys[1], (TOKENS, D), 1.0, 6.0, ((0, 128),))
    combine = jnp.clip(jnp.exp(math.log(0.3) - 2.7080503 * jax.random.uniform(arg_keys[2], (TOKENS, TOP), jnp.float32) ** block_levels(arg_keys[2], (TOKENS, TOP), ((0, 128),), -0.2, 0.2)), 0.02, 0.3)
    expert_ids_keys = jax.random.split(jax.random.fold_in(arg_keys[3], 1), TOKENS // TOK_DEV)
    expert_ids_turns = jax.random.permutation(jax.random.fold_in(arg_keys[3], 3), TOKENS // TOK_DEV)
    expert_ids = jax.vmap(lambda own, number: deal_out(jax.random.fold_in(arg_keys[3], 2), own, number, TOK_DEV, EXPERTS, TOP, CAPS, 2))(expert_ids_keys, expert_ids_turns).reshape((TOKENS, TOP))
    w_gate = centred(arg_keys[4], (EXPERTS, D, FF), D ** -0.5, 0.125, ((0, 64), (1, 2)))
    w_up = centred(arg_keys[5], (EXPERTS, D, FF), D ** -0.5, 0.125, ((0, 64), (1, 2)))
    w_down = centred(arg_keys[6], (EXPERTS, D, FF), FF ** -0.5, 0.15625, ((0, 64), (1, 2)))
    return {"tokens": tokens, "grad_out": grad_out, "combine": combine, "expert_ids": expert_ids, "w_gate": w_gate, "w_up": w_up, "w_down": w_down}


def expert_backward(expert_in, expert_grad_in, gate_mat, up_mat, down_mat):
    gate_pre = jnp.dot(expert_in, gate_mat, preferred_element_type=jnp.float32)
    up_pre = jnp.dot(expert_in, up_mat, preferred_element_type=jnp.float32)
    sigmoid_gate = jax.nn.sigmoid(gate_pre)
    gate_act = gate_pre * sigmoid_gate
    hidden = (gate_act * up_pre).astype(jnp.bfloat16)
    grad_hidden = jnp.dot(expert_grad_in, down_mat, preferred_element_type=jnp.float32)
    grad_gate = (grad_hidden * up_pre * sigmoid_gate * (1.0 + gate_pre * (1.0 - sigmoid_gate))).astype(jnp.bfloat16)
    grad_up = (grad_hidden * gate_act).astype(jnp.bfloat16)
    contract = (((1,), (1,)), ((), ()))
    grad_x = lax.dot_general(grad_gate, gate_mat, contract, preferred_element_type=jnp.float32)
    grad_x = grad_x + lax.dot_general(grad_up, up_mat, contract, preferred_element_type=jnp.float32)
    return hidden, grad_gate, grad_up, grad_x.astype(jnp.bfloat16)


def replica_terms(expert_in, expert_grad_in, hidden, grad_gate, grad_up):
    contract = (((0,), (0,)), ((), ()))
    terms = jnp.concatenate([
        lax.dot_general(expert_in, grad_gate, contract, preferred_element_type=jnp.float32),
        lax.dot_general(expert_in, grad_up, contract, preferred_element_type=jnp.float32),
        lax.dot_general(expert_grad_in, hidden, contract, preferred_element_type=jnp.float32)], axis=1)
    rounded = lax.optimization_barrier(terms.astype(jnp.bfloat16))
    return rounded.astype(jnp.float32)


def reference(tokens, grad_out, combine, expert_ids, w_gate, w_up, w_down):
    blocks = N_DP * N_EXPERT
    assigns = TOK_DEV * TOP
    slot_rows = EXPERTS * CAPS
    block_ids = expert_ids.reshape(blocks, assigns)
    onehot = (block_ids[:, :, None] == jnp.arange(EXPERTS, dtype=jnp.int32)[None, None, :]).astype(jnp.int32)
    before = jnp.cumsum(onehot, axis=1) - onehot
    slot_rank = jnp.sum(before * onehot, axis=2).astype(jnp.int32)
    position = (block_ids * CAPS + slot_rank).astype(jnp.int32)
    block_num = jnp.broadcast_to(jnp.arange(blocks, dtype=jnp.int32)[:, None], (blocks, assigns))
    assign_order = jnp.broadcast_to(jnp.arange(assigns, dtype=jnp.int32)[None, :], (blocks, assigns))
    slot_table = jnp.full((blocks, slot_rows), -1, jnp.int32).at[block_num, position].set(assign_order)
    filled = slot_table >= 0
    safe_entry = jnp.where(filled, slot_table, 0).astype(jnp.int32)
    block_base = jnp.arange(blocks, dtype=jnp.int32)[:, None] * TOK_DEV
    token_index = jnp.where(filled, block_base + safe_entry // TOP, TOKENS).astype(jnp.int32)
    flat_combine = combine.reshape(blocks, assigns)
    weight = jnp.where(filled, jnp.take_along_axis(flat_combine, safe_entry, axis=1), jnp.zeros_like(flat_combine[:, :1]))
    token_index = token_index.reshape(N_DP, EXPERTS, EXPERTS, CAPS).transpose(0, 2, 1, 3).reshape(N_DP, EXPERTS, slot_rows)
    weight = weight.reshape(N_DP, EXPERTS, EXPERTS, CAPS).transpose(0, 2, 1, 3).reshape(N_DP, EXPERTS, slot_rows)
    padded_tokens = jnp.concatenate([tokens, jnp.zeros((1, D), jnp.bfloat16)], axis=0)
    padded_grad = jnp.concatenate([grad_out, jnp.zeros((1, D), jnp.bfloat16)], axis=0)

    def expert_step(summed, expert):
        rows_of = token_index[:, expert]
        weight_of = weight[:, expert]
        gate_mat = w_gate[expert]
        up_mat = w_up[expert]
        down_mat = w_down[expert]
        partials = jnp.zeros((D, 3 * FF), jnp.float32)
        for replica in range(N_DP):
            expert_in = padded_tokens[rows_of[replica]]
            expert_grad_in = (weight_of[replica][:, None] * padded_grad[rows_of[replica]].astype(jnp.float32)).astype(jnp.bfloat16)
            hidden, grad_gate, grad_up, grad_x = expert_backward(expert_in, expert_grad_in, gate_mat, up_mat, down_mat)
            summed = summed.at[rows_of[replica]].add(grad_x.astype(jnp.float32))
            partials = partials + replica_terms(expert_in, expert_grad_in, hidden, grad_gate, grad_up)
        return summed, partials.astype(jnp.bfloat16)

    initial = jnp.zeros((TOKENS + 1, D), jnp.float32)
    summed, grads = lax.scan(expert_step, initial, jnp.arange(EXPERTS, dtype=jnp.int32))
    token_grad = summed[:TOKENS].astype(jnp.bfloat16)
    return token_grad, grads[:, :, :FF], grads[:, :, FF:2 * FF], grads[:, :, 2 * FF:]
```

```python
import functools

import jax
import jax.numpy as jnp
from jax import lax
from jax.experimental import pallas as pl
from jax.experimental.pallas import tpu as pltpu
from jax.sharding import PartitionSpec as P

MESH = pl.DeviceIdType.MESH
F32, BF16 = jnp.float32, jnp.bfloat16

TOK, TOP, D, FF = 64, 8, 1792, 1280
HALF = D // 2
CH = 256
CHUNKS = 3
IN_COLS = ((0, 640), (640, 1280), (1280, 1792))
GR_COLS = ((0, 512), (512, 1152), (1152, 1792))
RT_COLS = ((0, 640), (640, 1152), (1152, 1792))
WI = tuple(b - a for a, b in IN_COLS)
WG = tuple(b - a for a, b in GR_COLS)
WR = tuple(b - a for a, b in RT_COLS)
WP = tuple(a + b for a, b in zip(WI, WG))


def expert_of(p, line, j):
    if p == 0:
        return line * 16 + j
    if p == 1:
        return (j // 4) * 16 + line * 4 + j % 4
    return j * 4 + line


def dot(a, b):
    return jnp.dot(a, b, preferred_element_type=F32)


def dot_nt(a, b):
    return lax.dot_general(a, b, (((1,), (1,)), ((), ())), preferred_element_type=F32)


def dot_tn(a, b):
    return lax.dot_general(a, b, (((0,), (0,)), ((), ())), preferred_element_type=F32)


def body(
    ids_ref, comb_ref, tok_ref, gout_ref, wg_ref, wu_ref, wd_ref,
    tg_ref, og_ref, ou_ref, od_ref,
    wfull, line0, line1, line2, mytab, mytabs, tabs, r_tab, c_tab, a_mat, perm,
    spk0, spk1, spk2, rx0, rx1, rx2, xin, gin, hid, gga, gup, gx,
    rs0, rs1, rs2, rr0, rr1, rr2, ls0, ls1, ls2, lr0, lr1, lr2,
    w_loc, w_send, w_recv, lt_send, lt_recv, x_send, x_recv, g_send, g_recv,
    d_send, d_recv, b_send, b_recv, l_send, l_recv, q_send, q_recv, free_sem,
):
    lines, spk, rx = (line0, line1, line2), (spk0, spk1, spk2), (rx0, rx1, rx2)
    rs, rr = (rs0, rs1, rs2), (rr0, rr1, rr2)
    ls, lr = (ls0, ls1, ls2), (lr0, lr1, lr2)
    w_in = (wg_ref, wu_ref, wd_ref)
    w_out = (og_ref, ou_ref, od_ref)
    d = lax.axis_index("dp")
    e = lax.axis_index("expert")
    z, y, x = e // 16, (e // 4) % 4, e % 4
    lcoord = (z, y, x)
    jcoord = (y * 4 + x, z * 4 + x, z * 4 + y)
    partner = (1 - d, e)

    def peer_j(p, i):
        j = jcoord[p]
        return ((j // 4 + i // 4) % 4) * 4 + (j % 4 + i % 4) % 4

    def remote(src, dst, ss, rsem, device):
        return pltpu.make_async_remote_copy(
            src_ref=src, dst_ref=dst, send_sem=ss, recv_sem=rsem,
            device_id=device, device_id_type=MESH,
        )

    barrier = pltpu.get_barrier_semaphore()

    def greet(i, carry):
        for p in range(3):
            pl.semaphore_signal(
                barrier, inc=1,
                device_id=(d, expert_of(p, lcoord[p], peer_j(p, i))), device_id_type=MESH,
            )
        return carry

    lax.fori_loop(1, 16, greet, 0)
    pl.semaphore_signal(barrier, inc=1, device_id=partner, device_id_type=MESH)

    own_rows = pl.ds(pl.multiple_of(d * HALF, HALF), HALF)
    for w in range(3):
        pltpu.make_async_copy(w_in[w].at[0], wfull.at[w, own_rows], w_loc.at[w]).start()

    ids = ids_ref[...].astype(F32)
    e_iota = lax.broadcasted_iota(jnp.int32, (64, TOK), 0).astype(F32)
    named = jnp.zeros((64, TOK), F32)
    for k in range(TOP):
        named = named + jnp.where(ids[k : k + 1, :] == e_iota, 1.0, 0.0)
    upper = (
        lax.broadcasted_iota(jnp.int32, (TOK, TOK), 0)
        < lax.broadcasted_iota(jnp.int32, (TOK, TOK), 1)
    )
    earlier = dot(named.astype(BF16), jnp.where(upper, 1.0, 0.0).astype(BF16))
    mytab[...] = jnp.zeros_like(mytab)
    mytab[0:8, 0:TOK] = ids
    for k in range(TOP):
        mytab[8 + k : 9 + k, 0:TOK] = jnp.sum(
            jnp.where(ids[k : k + 1, :] == e_iota, earlier, 0.0), axis=0, keepdims=True
        )
    mytab[16:24, 0:TOK] = comb_ref[...]
    low = mytab[...]
    high = pltpu.roll(low, 64, 1)
    for p in range(3):
        mytabs[p] = jnp.where(lcoord[p] % 2 == 0, low, high)

    pl.semaphore_wait(barrier, 46)

    for i in range(1, 4):
        for p in range(3):
            to = (d, expert_of(p, (lcoord[p] + i) % 4, jcoord[p]))
            rows = pl.ds(pl.multiple_of(lcoord[p] * TOK, TOK), TOK)
            remote(mytabs.at[p], tabs.at[p, lcoord[p]], lt_send.at[p], lt_recv.at[p], to).start()
            remote(
                tok_ref.at[:, pl.ds(IN_COLS[p][0], WI[p])],
                lines[p].at[rows, pl.ds(0, WI[p])],
                x_send.at[p], x_recv.at[p], to,
            ).start()
            remote(
                gout_ref.at[:, pl.ds(GR_COLS[p][0], WG[p])],
                lines[p].at[rows, pl.ds(WI[p], WG[p])],
                g_send.at[p], g_recv.at[p], to,
            ).start()
    for w in range(3):
        remote(w_in[w].at[0], wfull.at[w, own_rows], w_send.at[w], w_recv.at[w], partner).start()

    for p in range(3):
        rows = pl.ds(pl.multiple_of(lcoord[p] * TOK, TOK), TOK)
        tabs[p, lcoord[p]] = mytabs[p]
        lines[p][rows, 0 : WI[p]] = tok_ref[:, IN_COLS[p][0] : IN_COLS[p][1]]
        lines[p][rows, WI[p] : WP[p]] = gout_ref[:, GR_COLS[p][0] : GR_COLS[p][1]]

    row0 = lax.broadcasted_iota(jnp.int32, (CH, CH), 0)
    col0 = lax.broadcasted_iota(jnp.int32, (CH, CH), 1)
    ry, rxx, rz, rk = (row0 >> 6) & 3, (row0 >> 4) & 3, (row0 >> 2) & 3, row0 & 3
    perm[0] = jnp.where(col0 == (rz << 6) + (rxx << 4) + (ry << 2) + rk, 1.0, 0.0).astype(BF16)
    perm[1] = jnp.where(col0 == (rz << 6) + (ry << 4) + (rxx << 2) + rk, 1.0, 0.0).astype(BF16)

    def line_wait(p):
        remote(tabs.at[p, pl.ds(0, 3)], tabs.at[p, pl.ds(0, 3)], lt_send.at[p], lt_recv.at[p], partner).wait_recv()
        a = lines[p].at[pl.ds(0, 192), pl.ds(0, WI[p])]
        b = lines[p].at[pl.ds(0, 192), pl.ds(WI[p], WG[p])]
        remote(a, a, x_send.at[p], x_recv.at[p], partner).wait_recv()
        remote(b, b, g_send.at[p], g_recv.at[p], partner).wait_recv()

    for p in range(3):
        line_wait(p)
        table = jnp.concatenate([tabs[p, 0] + tabs[p, 1], tabs[p, 2] + tabs[p, 3]], axis=1)
        jj = lax.broadcasted_iota(jnp.int32, (16, 1), 0)
        if p == 0:
            code = jj + lcoord[0] * 16
        elif p == 1:
            code = ((jj >> 2) << 4) + (jj & 3) + lcoord[1] * 4
        else:
            code = (jj << 2) + lcoord[2]
        code = code.astype(F32)
        rank = jnp.zeros((16, CH), F32)
        weight = jnp.zeros((16, CH), F32)
        for k in range(TOP):
            here = table[k : k + 1, :] == code
            rank = rank + jnp.where(here, table[8 + k : 9 + k, :] + 1.0, 0.0)
            weight = weight + jnp.where(here, table[16 + k : 17 + k, :], 0.0)
        r_tab[p] = rank - 1.0
        c_tab[p] = weight

    def pack(c, carry):
        crow = pl.multiple_of(c * CH, CH)
        r_i = lax.broadcasted_iota(jnp.int32, (CH, CH), 0)
        s_i = lax.broadcasted_iota(jnp.int32, (CH, CH), 1) >> 6
        want = jnp.where(((r_i >> 2) & 3) == s_i, (r_i & 3) + 4 * c, -100).astype(F32)
        for p in range(3):
            rank = jnp.broadcast_to(r_tab[p][:, None, :], (16, 16, CH)).reshape(CH, CH)
            wt = jnp.broadcast_to(c_tab[p][:, None, :], (16, 16, CH)).reshape(CH, CH)
            hit = rank == want
            one = jnp.where(hit, 1.0, 0.0).astype(BF16)
            a_mat[p, pl.ds(crow, CH), :] = one
            w_row = jnp.sum(jnp.where(hit, wt, 0.0), axis=1, keepdims=True)
            spk[p][pl.ds(crow, CH), 0 : WI[p]] = dot(one, lines[p][:, 0 : WI[p]]).astype(BF16)
            spk[p][pl.ds(crow, CH), WI[p] : WP[p]] = (
                dot(one, lines[p][:, WI[p] : WP[p]]) * w_row
            ).astype(BF16)

        def send(i, carry2):
            for p in range(3):
                jj = peer_j(p, i)
                to = (d, expert_of(p, lcoord[p], jj))
                remote(
                    spk[p].at[pl.ds(pl.multiple_of(crow + jj * 16, 16), 16)],
                    rx[p].at[pl.ds(pl.multiple_of(crow + jcoord[p] * 16, 16), 16)],
                    d_send.at[p, c], d_recv.at[p, c], to,
                ).start()
            return carry2

        lax.fori_loop(1, 16, send, 0)
        for p in range(3):
            mine = pl.ds(pl.multiple_of(crow + jcoord[p] * 16, 16), 16)
            rx[p][mine, :] = spk[p][mine, :]
        return carry

    lax.fori_loop(0, CHUNKS, pack, 0)

    for w in range(3):
        pltpu.make_async_copy(w_in[w].at[0], wfull.at[w, own_rows], w_loc.at[w]).wait()
        remote(w_in[w].at[0], wfull.at[w, own_rows], w_send.at[w], w_recv.at[w], partner).wait()

    def compute(c, carry):
        crow = pl.multiple_of(c * CH, CH)
        rows = pl.ds(crow, CH)
        for p in range(3):
            part = rx[p].at[pl.ds(0, 240)]
            remote(part, part, d_send.at[p, c], d_recv.at[p, c], partner).wait_recv()
        for p in range(3):
            if p == 0:
                xin[rows, IN_COLS[0][0] : IN_COLS[0][1]] = rx[0][rows, 0 : WI[0]]
                gin[rows, GR_COLS[0][0] : GR_COLS[0][1]] = rx[0][rows, WI[0] : WP[0]]
            else:
                xin[rows, IN_COLS[p][0] : IN_COLS[p][1]] = dot(
                    perm[p - 1], rx[p][rows, 0 : WI[p]]
                ).astype(BF16)
                gin[rows, GR_COLS[p][0] : GR_COLS[p][1]] = dot(
                    perm[p - 1], rx[p][rows, WI[p] : WP[p]]
                ).astype(BF16)

        def units(n, carry2):
            cols = pl.ds(pl.multiple_of(n * 256, 256), 256)
            gate = dot(xin[rows, :], wfull[0, :, cols])
            up = dot(xin[rows, :], wfull[1, :, cols])
            gh = dot(gin[rows, :], wfull[2, :, cols])
            sig = jax.nn.sigmoid(gate)
            act = gate * sig
            hid[rows, cols] = (act * up).astype(BF16)
            gga[rows, cols] = (gh * up * sig * (1.0 + gate * (1.0 - sig))).astype(BF16)
            gup[rows, cols] = (gh * act).astype(BF16)
            return carry2

        lax.fori_loop(0, FF // 256, units, 0)

        def grads(n, carry2):
            cols = pl.ds(pl.multiple_of(n * 256, 256), 256)
            gx[:, cols] = (
                dot_nt(gga[rows, :], wfull[0, cols, :]) + dot_nt(gup[rows, :], wfull[1, cols, :])
            ).astype(BF16)
            return carry2

        lax.fori_loop(0, D // 256, grads, 0)
        for p in range(3):
            cols = gx[:, RT_COLS[p][0] : RT_COLS[p][1]]
            rs[p][rows, :] = cols if p == 0 else dot_tn(perm[p - 1], cols).astype(BF16)

        def send(i, carry2):
            for p in range(3):
                jj = peer_j(p, i)
                to = (d, expert_of(p, lcoord[p], jj))
                remote(
                    rs[p].at[pl.ds(pl.multiple_of(crow + jj * 16, 16), 16)],
                    rr[p].at[pl.ds(pl.multiple_of(crow + jcoord[p] * 16, 16), 16)],
                    b_send.at[p, c], b_recv.at[p, c], to,
                ).start()
            return carry2

        lax.fori_loop(1, 16, send, 0)
        for p in range(3):
            mine = pl.ds(pl.multiple_of(crow + jcoord[p] * 16, 16), 16)
            rr[p][mine, :] = rs[p][mine, :]
        return carry

    lax.fori_loop(0, CHUNKS, compute, 0)
    pl.semaphore_signal(free_sem, inc=1, device_id=partner, device_id_type=MESH)

    far = (1 - d) * HALF
    near = d * HALF

    def far_terms(n, carry):
        cols = pl.ds(pl.multiple_of(n * 256, 256), 256)
        half = pl.ds(pl.multiple_of(far, 128), HALF)
        wfull[0, 0:HALF, cols] = dot_tn(xin[:, half], gga[:, cols]).astype(BF16)
        wfull[1, 0:HALF, cols] = dot_tn(xin[:, half], gup[:, cols]).astype(BF16)
        wfull[2, 0:HALF, cols] = dot_tn(gin[:, half], hid[:, cols]).astype(BF16)
        for w in range(3):
            remote(
                wfull.at[w, pl.ds(0, HALF), cols], wfull.at[w, pl.ds(HALF, HALF), cols],
                q_send.at[n], q_recv.at[n], partner,
            ).start()
        return carry

    pl.semaphore_wait(free_sem, 1)
    lax.fori_loop(0, FF // 256, far_terms, 0)

    for p in range(3):
        for c in range(CHUNKS):
            part = rr[p].at[pl.ds(0, 240)]
            remote(part, part, b_send.at[p, c], b_recv.at[p, c], partner).wait_recv()
        ls[p][...] = dot_tn(a_mat[p], rr[p][...]).astype(BF16)
        for i in range(1, 4):
            s = (lcoord[p] + i) % 4
            to = (d, expert_of(p, s, jcoord[p]))
            remote(
                ls[p].at[pl.ds(pl.multiple_of(s * TOK, TOK), TOK)],
                lr[p].at[lcoord[p]],
                l_send.at[p], l_recv.at[p], to,
            ).start()
        lr[p][lcoord[p]] = ls[p][pl.ds(pl.multiple_of(lcoord[p] * TOK, TOK), TOK), :]

    def near_terms(n, carry):
        cols = pl.ds(pl.multiple_of(n * 256, 256), 256)
        half = pl.ds(pl.multiple_of(near, 128), HALF)
        terms = (
            dot_tn(xin[:, half], gga[:, cols]),
            dot_tn(xin[:, half], gup[:, cols]),
            dot_tn(gin[:, half], hid[:, cols]),
        )
        part = wfull.at[pl.ds(0, 3), pl.ds(HALF, HALF), cols]
        remote(part, part, q_send.at[n], q_recv.at[n], partner).wait_recv()
        for w in range(3):
            other = wfull[w, HALF:D, cols].astype(F32)
            w_out[w][0, :, cols] = (terms[w].astype(BF16).astype(F32) + other).astype(BF16)
        return carry

    lax.fori_loop(0, FF // 256, near_terms, 0)

    for p in range(3):
        part = lr[p].at[pl.ds(0, 3)]
        remote(part, part, l_send.at[p], l_recv.at[p], partner).wait_recv()
        total = lr[p][0].astype(F32) + lr[p][1].astype(F32)
        total = total + lr[p][2].astype(F32) + lr[p][3].astype(F32)
        tg_ref[:, RT_COLS[p][0] : RT_COLS[p][1]] = total.astype(BF16)

    for p in range(3):
        remote(tabs.at[p, pl.ds(0, 3)], tabs.at[p, pl.ds(0, 3)], lt_send.at[p], lt_recv.at[p], partner).wait_send()
        a = lines[p].at[pl.ds(0, 192), pl.ds(0, WI[p])]
        b = lines[p].at[pl.ds(0, 192), pl.ds(WI[p], WG[p])]
        remote(a, a, x_send.at[p], x_recv.at[p], partner).wait_send()
        remote(b, b, g_send.at[p], g_recv.at[p], partner).wait_send()
        for c in range(CHUNKS):
            part = rx[p].at[pl.ds(0, 240)]
            remote(part, part, d_send.at[p, c], d_recv.at[p, c], partner).wait_send()
            part = rr[p].at[pl.ds(0, 240)]
            remote(part, part, b_send.at[p, c], b_recv.at[p, c], partner).wait_send()
        part = lr[p].at[pl.ds(0, 3)]
        remote(part, part, l_send.at[p], l_recv.at[p], partner).wait_send()
    for n in range(FF // 256):
        part = wfull.at[pl.ds(0, 3), pl.ds(0, HALF), pl.ds(n * 256, 256)]
        remote(part, part, q_send.at[n], q_recv.at[n], partner).wait_send()


def shards(tokens, grad_out, combine, expert_ids, w_gate, w_up, w_down):
    vm, hbm = pl.BlockSpec(memory_space=pltpu.VMEM), pl.BlockSpec(memory_space=pl.ANY)
    rows = CHUNKS * CH
    v = pltpu.VMEM
    scratch = [
        v((3, D, FF), BF16),
        *[v((CH, w), BF16) for w in WP],
        v((24, 128), F32), v((3, 24, 128), F32), v((3, 4, 24, 128), F32),
        v((3, 16, CH), F32), v((3, 16, CH), F32),
        v((3, rows, CH), BF16), v((2, CH, CH), BF16),
        *[v((rows, w), BF16) for w in WP],
        *[v((rows, w), BF16) for w in WP],
        v((rows, D), BF16), v((rows, D), BF16),
        v((rows, FF), BF16), v((rows, FF), BF16), v((rows, FF), BF16),
        v((CH, D), BF16),
        *[v((rows, w), BF16) for w in WR],
        *[v((rows, w), BF16) for w in WR],
        *[v((CH, w), BF16) for w in WR],
        *[v((4, TOK, w), BF16) for w in WR],
    ]
    dma = pltpu.SemaphoreType.DMA
    sems = [
        *[dma((3,))] * 9,
        *[dma((3, 3))] * 4,
        *[dma((3,))] * 2,
        *[dma((FF // 256,))] * 2,
        pltpu.SemaphoreType.REGULAR,
    ]
    wshape = jax.ShapeDtypeStruct((1, HALF, FF), BF16)
    return pl.pallas_call(
        body,
        out_shape=(jax.ShapeDtypeStruct((TOK, D), BF16), wshape, wshape, wshape),
        in_specs=[vm, vm, vm, vm, hbm, hbm, hbm],
        out_specs=(vm, vm, vm, vm),
        scratch_shapes=scratch + sems,
        compiler_params=pltpu.CompilerParams(
            collective_id=0, has_side_effects=True, vmem_limit_bytes=67043328
        ),
        name="routed_backward",
    )(expert_ids.T, combine.T, tokens, grad_out, w_gate, w_up, w_down)


def solution(mesh):
    rows = P(("dp", "expert"), None)
    weights = P("expert", "dp", None)
    return jax.shard_map(
        shards,
        mesh=mesh,
        in_specs=(rows, rows, rows, rows, weights, weights, weights),
        out_specs=(rows, weights, weights, weights),
        check_vma=False,
    )
```

```python
import functools

import jax
import jax.numpy as jnp
from jax import lax
from jax.experimental import pallas as pl
from jax.experimental.pallas import tpu as pltpu
from jax.sharding import PartitionSpec as P

MESH = pl.DeviceIdType.MESH
F32, BF16 = jnp.float32, jnp.bfloat16

TOK, TOP, D, FF = 64, 8, 1792, 1280
HALF = D // 2
CH = 256
CHUNKS = 3
TILES = FF // 256
IN_COLS = ((0, 640), (640, 1280), (1280, 1792))
GR_COLS = ((0, 512), (512, 1152), (1152, 1792))
RT_COLS = ((0, 640), (640, 1152), (1152, 1792))
WI = tuple(b - a for a, b in IN_COLS)
WG = tuple(b - a for a, b in GR_COLS)
WR = tuple(b - a for a, b in RT_COLS)
WP = tuple(a + b for a, b in zip(WI, WG))


def expert_of(p, line, j):
    if p == 0:
        return line * 16 + j
    if p == 1:
        return (j // 4) * 16 + line * 4 + j % 4
    return j * 4 + line


def dot(a, b):
    return jnp.dot(a, b, preferred_element_type=F32)


def dot_nt(a, b):
    return lax.dot_general(a, b, (((1,), (1,)), ((), ())), preferred_element_type=F32)


def dot_tn(a, b):
    return lax.dot_general(a, b, (((0,), (0,)), ((), ())), preferred_element_type=F32)


def body(
    ids_hbm, comb_hbm, tok_hbm, gout_hbm, wg_ref, wu_ref, wd_ref,
    tg_ref, og_ref, ou_ref, od_ref,
    ids_ref, comb_ref, tok_ref, gout_ref, wfull, line0, line1, line2, mytab, mytabs, tabs, r_tab, c_tab, a_mat, perm,
    spk0, spk1, spk2, rx0, rx1, rx2, xg, hg, far_xg, far_hg, gx,
    rr0, rr1, rr2, lr0, lr1, lr2,
    i_loc, w_loc, w_send, w_recv, lt_send, lt_recv, x_send, x_recv, g_send, g_recv,
    d_send, d_recv, b_send, b_recv, l_send, l_recv, q_send, q_recv, h_send, h_recv,
):
    lines, spk, rx = (line0, line1, line2), (spk0, spk1, spk2), (rx0, rx1, rx2)
    rr = (rr0, rr1, rr2)
    lr = (lr0, lr1, lr2)
    w_in = (wg_ref, wu_ref, wd_ref)
    w_out = (og_ref, ou_ref, od_ref)
    d = lax.axis_index("dp")
    e = lax.axis_index("expert")
    z, y, x = e // 16, (e // 4) % 4, e % 4
    lcoord = (z, y, x)
    jcoord = (y * 4 + x, z * 4 + x, z * 4 + y)
    partner = (1 - d, e)

    def peer_j(p, i):
        j = jcoord[p]
        return ((j // 4 + i // 4) % 4) * 4 + (j % 4 + i % 4) % 4

    def remote(src, dst, ss, rsem, device):
        return pltpu.make_async_remote_copy(
            src_ref=src, dst_ref=dst, send_sem=ss, recv_sem=rsem,
            device_id=device, device_id_type=MESH,
        )

    small = ((ids_hbm, ids_ref), (comb_hbm, comb_ref), (tok_hbm, tok_ref), (gout_hbm, gout_ref))
    for k, (src, dst) in enumerate(small):
        pltpu.make_async_copy(src, dst, i_loc.at[k]).start()

    barrier = pltpu.get_barrier_semaphore()

    def greet(p, i):
        pl.semaphore_signal(
            barrier, inc=1,
            device_id=(d, expert_of(p, lcoord[p], peer_j(p, i))), device_id_type=MESH,
        )

    for i in range(1, 16):
        greet(0, i)
        if i >= 4:
            greet(1, i)
            if i % 4:
                greet(2, i)
    pl.semaphore_signal(barrier, inc=1, device_id=partner, device_id_type=MESH)

    own_rows = pl.ds(pl.multiple_of(d * HALF, HALF), HALF)
    for w in range(3):
        pltpu.make_async_copy(w_in[w].at[0], wfull.at[w, own_rows], w_loc.at[w]).start()

    for k, (src, dst) in enumerate(small):
        pltpu.make_async_copy(src, dst, i_loc.at[k]).wait()
    ids = ids_ref[...].astype(F32)
    e_iota = lax.broadcasted_iota(jnp.int32, (64, TOK), 0).astype(F32)
    named = jnp.zeros((64, TOK), F32)
    for k in range(TOP):
        named = named + jnp.where(ids[k : k + 1, :] == e_iota, 1.0, 0.0)
    upper = (
        lax.broadcasted_iota(jnp.int32, (TOK, TOK), 0)
        < lax.broadcasted_iota(jnp.int32, (TOK, TOK), 1)
    )
    earlier = dot(named.astype(BF16), jnp.where(upper, 1.0, 0.0).astype(BF16))
    mytab[...] = jnp.zeros_like(mytab)
    mytab[0:8, 0:TOK] = ids
    for k in range(TOP):
        mytab[8 + k : 9 + k, 0:TOK] = jnp.sum(
            jnp.where(ids[k : k + 1, :] == e_iota, earlier, 0.0), axis=0, keepdims=True
        )
    mytab[16:24, 0:TOK] = comb_ref[...]
    low = mytab[...]
    high = pltpu.roll(low, 64, 1)
    for p in range(3):
        mytabs[p] = jnp.where(lcoord[p] % 2 == 0, low, high)

    pl.semaphore_wait(barrier, 37)

    for i in range(1, 4):
        for p in range(3):
            to = (d, expert_of(p, (lcoord[p] + i) % 4, jcoord[p]))
            rows = pl.ds(pl.multiple_of(lcoord[p] * TOK, TOK), TOK)
            remote(mytabs.at[p], tabs.at[p, lcoord[p]], lt_send.at[p], lt_recv.at[p], to).start()
            remote(
                tok_ref.at[:, pl.ds(IN_COLS[p][0], WI[p])],
                lines[p].at[rows, pl.ds(0, WI[p])],
                x_send.at[p], x_recv.at[p], to,
            ).start()
            remote(
                gout_ref.at[:, pl.ds(GR_COLS[p][0], WG[p])],
                lines[p].at[rows, pl.ds(WI[p], WG[p])],
                g_send.at[p], g_recv.at[p], to,
            ).start()
    for w in range(3):
        remote(w_in[w].at[0], wfull.at[w, own_rows], w_send.at[w], w_recv.at[w], partner).start()

    for p in range(3):
        rows = pl.ds(pl.multiple_of(lcoord[p] * TOK, TOK), TOK)
        tabs[p, lcoord[p]] = mytabs[p]
        lines[p][rows, 0 : WI[p]] = tok_ref[:, IN_COLS[p][0] : IN_COLS[p][1]]
        lines[p][rows, WI[p] : WP[p]] = gout_ref[:, GR_COLS[p][0] : GR_COLS[p][1]]

    row0 = lax.broadcasted_iota(jnp.int32, (CH, CH), 0)
    col0 = lax.broadcasted_iota(jnp.int32, (CH, CH), 1)
    ry, rxx, rz, rk = (row0 >> 6) & 3, (row0 >> 4) & 3, (row0 >> 2) & 3, row0 & 3
    perm[0] = jnp.where(col0 == (rz << 6) + (rxx << 4) + (ry << 2) + rk, 1.0, 0.0).astype(BF16)
    perm[1] = jnp.where(col0 == (rz << 6) + (ry << 4) + (rxx << 2) + rk, 1.0, 0.0).astype(BF16)
    perm[2] = jnp.where(col0 == row0, 1.0, 0.0).astype(BF16)
    perm[3] = jnp.where(col0 == (rxx << 6) + (rz << 4) + (ry << 2) + rk, 1.0, 0.0).astype(BF16)

    def line_wait(p):
        remote(tabs.at[p, pl.ds(0, 3)], tabs.at[p, pl.ds(0, 3)], lt_send.at[p], lt_recv.at[p], partner).wait_recv()
        a = lines[p].at[pl.ds(0, 192), pl.ds(0, WI[p])]
        b = lines[p].at[pl.ds(0, 192), pl.ds(WI[p], WG[p])]
        remote(a, a, x_send.at[p], x_recv.at[p], partner).wait_recv()
        remote(b, b, g_send.at[p], g_recv.at[p], partner).wait_recv()

    for p in range(3):
        line_wait(p)
        table = jnp.concatenate([tabs[p, 0] + tabs[p, 1], tabs[p, 2] + tabs[p, 3]], axis=1)
        jj = lax.broadcasted_iota(jnp.int32, (16, 1), 0)
        if p == 0:
            code = jj + lcoord[0] * 16
        elif p == 1:
            code = ((jj >> 2) << 4) + (jj & 3) + lcoord[1] * 4
        else:
            code = (jj << 2) + lcoord[2]
        code = code.astype(F32)
        rank = jnp.zeros((16, CH), F32)
        weight = jnp.zeros((16, CH), F32)
        for k in range(TOP):
            here = table[k : k + 1, :] == code
            rank = rank + jnp.where(here, table[8 + k : 9 + k, :] + 1.0, 0.0)
            weight = weight + jnp.where(here, table[16 + k : 17 + k, :], 0.0)
        r_tab[p] = rank - 1.0
        c_tab[p] = weight

    def dispatch(c):
        crow = c * CH

        def send(i, carry2):
            for p in range(3):
                jj = peer_j(p, i)
                to = (d, expert_of(p, lcoord[p], jj))
                remote(
                    spk[p].at[pl.ds(pl.multiple_of(crow + jj * 16, 16), 16)],
                    rx[p].at[pl.ds(pl.multiple_of(crow + jcoord[p] * 16, 16), 16)],
                    d_send.at[p, c], d_recv.at[p, c], to,
                ).start()
            return carry2

        lax.fori_loop(1, 16, send, 0)
        for p in range(3):
            mine = pl.ds(pl.multiple_of(crow + jcoord[p] * 16, 16), 16)
            rx[p][mine, :] = spk[p][mine, :]

    def give_back(c):
        crow = c * CH

        def send(i, carry2):
            for p in range(3):
                jj = peer_j(p, i)
                to = (d, expert_of(p, lcoord[p], jj))
                remote(
                    spk[p].at[pl.ds(pl.multiple_of(crow + jj * 16, 16), 16), pl.ds(0, WR[p])],
                    rr[p].at[pl.ds(pl.multiple_of(crow + jcoord[p] * 16, 16), 16)],
                    b_send.at[p, c], b_recv.at[p, c], to,
                ).start()
            return carry2

        lax.fori_loop(1, 16, send, 0)
        for p in range(3):
            mine = pl.ds(pl.multiple_of(crow + jcoord[p] * 16, 16), 16)
            rr[p][mine, :] = spk[p][mine, 0 : WR[p]]

    def pack(c, carry):
        crow = pl.multiple_of(c * CH, CH)
        r_i = lax.broadcasted_iota(jnp.int32, (CH, CH), 0)
        s_i = lax.broadcasted_iota(jnp.int32, (CH, CH), 1) >> 6
        want = jnp.where(((r_i >> 2) & 3) == s_i, (r_i & 3) + 4 * c, -100).astype(F32)
        for p in range(3):
            rank = jnp.broadcast_to(r_tab[p][:, None, :], (16, 16, CH)).reshape(CH, CH)
            wt = jnp.broadcast_to(c_tab[p][:, None, :], (16, 16, CH)).reshape(CH, CH)
            hit = rank == want
            one = jnp.where(hit, 1.0, 0.0).astype(BF16)
            a_mat[p, pl.ds(crow, CH), :] = one
            w_row = jnp.sum(jnp.where(hit, wt, 0.0), axis=1, keepdims=True)
            spk[p][pl.ds(crow, CH), 0 : WI[p]] = dot(one, lines[p][:, 0 : WI[p]]).astype(BF16)
            spk[p][pl.ds(crow, CH), WI[p] : WP[p]] = (
                dot(one, lines[p][:, WI[p] : WP[p]]) * w_row
            ).astype(BF16)

        @pl.when(c < 2)
        def _():
            dispatch(c)

        return carry

    lax.fori_loop(0, CHUNKS, pack, 0)

    def clear(n, carry):
        rows = pl.ds(pl.multiple_of(n * 128, 128), 128)
        for w in range(3):
            w_out[w][0, rows, :] = jnp.zeros((128, FF), F32)
        return carry

    lax.fori_loop(0, HALF // 128, clear, 0)

    for w in range(3):
        pltpu.make_async_copy(w_in[w].at[0], wfull.at[w, own_rows], w_loc.at[w]).wait()
        remote(w_in[w].at[0], wfull.at[w, own_rows], w_send.at[w], w_recv.at[w], partner).wait()

    near = pl.ds(pl.multiple_of(d * HALF, 128), HALF)
    far = pl.ds(pl.multiple_of((1 - d) * HALF, 128), HALF)

    def far_wait(c):
        remote(far_xg.at[c], far_xg.at[c], q_send.at[c], q_recv.at[c], partner).wait_recv()
        remote(far_hg.at[c], far_hg.at[c], h_send.at[c], h_recv.at[c], partner).wait_recv()

    def terms(c, n, carry):
        b = c % 2
        cols = pl.ds(pl.multiple_of(n * 256, 256), 256)
        for w in range(3):
            k = w // 2
            w_out[w][0, :, cols] += dot_tn(xg[b, k, :, near], hg[b, w, :, cols]) + dot_tn(
                far_xg[c, k], far_hg[c, w, :, cols]
            )
        return carry

    def compute(c, carry):
        crow = pl.multiple_of(c * CH, CH)
        rows = pl.ds(crow, CH)
        b = c % 2

        @pl.when(c >= 2)
        def _():
            remote(far_xg.at[c - 2], far_xg.at[c - 2], q_send.at[c - 2], q_recv.at[c - 2], partner).wait_send()
            remote(far_hg.at[c - 2], far_hg.at[c - 2], h_send.at[c - 2], h_recv.at[c - 2], partner).wait_send()

        for p in range(3):
            part = rx[p].at[pl.ds(0, 240)]
            remote(part, part, d_send.at[p, c], d_recv.at[p, c], partner).wait_recv()

        @pl.when(c >= 1)
        def _():
            give_back(c - 1)

        for p in range(3):
            i0, i1 = IN_COLS[p]
            g0, g1 = GR_COLS[p]
            if p == 0:
                xg[b, 0, :, i0:i1] = rx[0][rows, 0 : WI[0]]
                xg[b, 1, :, g0:g1] = rx[0][rows, WI[0] : WP[0]]
            else:
                xg[b, 0, :, i0:i1] = dot(perm[p - 1], rx[p][rows, 0 : WI[p]]).astype(BF16)
                xg[b, 1, :, g0:g1] = dot(perm[p - 1], rx[p][rows, WI[p] : WP[p]]).astype(BF16)
        for k in range(2):
            remote(
                xg.at[b, k, :, far], far_xg.at[c, k], q_send.at[c], q_recv.at[c], partner
            ).start()

        def units(n, carry2):
            cols = pl.ds(pl.multiple_of(n * 256, 256), 256)
            gate = dot(xg[b, 0], wfull[0, :, cols])
            up = dot(xg[b, 0], wfull[1, :, cols])
            gh = dot(xg[b, 1], wfull[2, :, cols])
            sig = jax.nn.sigmoid(gate)
            act = gate * sig
            hg[b, 2, :, cols] = (act * up).astype(BF16)
            hg[b, 0, :, cols] = (gh * up * sig * (1.0 + gate * (1.0 - sig))).astype(BF16)
            hg[b, 1, :, cols] = (gh * act).astype(BF16)
            return carry2

        lax.fori_loop(0, TILES, units, 0)

        @pl.when(c == 0)
        def _():
            dispatch(2)

        for k in range(3):
            remote(hg.at[b, k], far_hg.at[c, k], h_send.at[c], h_recv.at[c], partner).start()

        def grads(n, carry2):
            cols = pl.ds(pl.multiple_of(n * 256, 256), 256)
            gx[cols, :] = (
                dot_nt(wfull[0, cols, :], hg[b, 0]) + dot_nt(wfull[1, cols, :], hg[b, 1])
            ).astype(BF16)
            return carry2

        lax.fori_loop(0, D // 256, grads, 0)
        for p in range(3):
            part = rx[p].at[pl.ds(0, 240)]
            remote(part, part, d_send.at[p, c], d_recv.at[p, c], partner).wait_send()
            back = perm[(2, 0, 3)[p]]
            spk[p][rows, 0 : WR[p]] = dot_nt(back, gx[RT_COLS[p][0] : RT_COLS[p][1], :]).astype(BF16)

        @pl.when(c == 0)
        def _():
            far_wait(c)
            lax.fori_loop(0, TILES, functools.partial(terms, c), 0)

        return carry

    lax.fori_loop(0, CHUNKS, compute, 0)
    give_back(CHUNKS - 1)
    far_wait(1)
    far_wait(2)

    def late_terms(i, carry):
        return terms(1 + i // TILES, i % TILES, carry)

    lax.fori_loop(0, TILES + 2, late_terms, 0)

    for p in range(3):
        for c in range(CHUNKS):
            part = rr[p].at[pl.ds(0, 240)]
            remote(part, part, b_send.at[p, c], b_recv.at[p, c], partner).wait_recv()
        lines[p][:, 0 : WR[p]] = dot_tn(a_mat[p], rr[p][...]).astype(BF16)
        for i in range(1, 4):
            s = (lcoord[p] + i) % 4
            to = (d, expert_of(p, s, jcoord[p]))
            remote(
                lines[p].at[pl.ds(pl.multiple_of(s * TOK, TOK), TOK), pl.ds(0, WR[p])],
                lr[p].at[lcoord[p]],
                l_send.at[p], l_recv.at[p], to,
            ).start()
        lr[p][lcoord[p]] = lines[p][
            pl.ds(pl.multiple_of(lcoord[p] * TOK, TOK), TOK), 0 : WR[p]
        ]

    lax.fori_loop(TILES + 2, 2 * TILES, late_terms, 0)

    for p in range(3):
        part = lr[p].at[pl.ds(0, 3)]
        remote(part, part, l_send.at[p], l_recv.at[p], partner).wait_recv()
        total = lr[p][0].astype(F32) + lr[p][1].astype(F32)
        total = total + lr[p][2].astype(F32) + lr[p][3].astype(F32)
        tg_ref[:, RT_COLS[p][0] : RT_COLS[p][1]] = total.astype(BF16)

    for p in range(3):
        remote(tabs.at[p, pl.ds(0, 3)], tabs.at[p, pl.ds(0, 3)], lt_send.at[p], lt_recv.at[p], partner).wait_send()
        a = lines[p].at[pl.ds(0, 192), pl.ds(0, WI[p])]
        b = lines[p].at[pl.ds(0, 192), pl.ds(WI[p], WG[p])]
        remote(a, a, x_send.at[p], x_recv.at[p], partner).wait_send()
        remote(b, b, g_send.at[p], g_recv.at[p], partner).wait_send()
        for c in range(CHUNKS):
            part = rr[p].at[pl.ds(0, 240)]
            remote(part, part, b_send.at[p, c], b_recv.at[p, c], partner).wait_send()
        part = lr[p].at[pl.ds(0, 3)]
        remote(part, part, l_send.at[p], l_recv.at[p], partner).wait_send()
    for c in range(1, CHUNKS):
        remote(far_xg.at[c], far_xg.at[c], q_send.at[c], q_recv.at[c], partner).wait_send()
        remote(far_hg.at[c], far_hg.at[c], h_send.at[c], h_recv.at[c], partner).wait_send()


def shards(tokens, grad_out, combine, expert_ids, w_gate, w_up, w_down):
    vm, hbm = pl.BlockSpec(memory_space=pltpu.VMEM), pl.BlockSpec(memory_space=pl.ANY)
    rows = CHUNKS * CH
    v = pltpu.VMEM
    scratch = [
        v((TOP, TOK), jnp.int32), v((TOP, TOK), F32), v((TOK, D), BF16), v((TOK, D), BF16),
        v((3, D, FF), BF16),
        *[v((CH, w), BF16) for w in WP],
        v((24, 128), F32), v((3, 24, 128), F32), v((3, 4, 24, 128), F32),
        v((3, 16, CH), F32), v((3, 16, CH), F32),
        v((3, rows, CH), BF16), v((4, CH, CH), BF16),
        *[v((rows, w), BF16) for w in WP],
        *[v((rows, w), BF16) for w in WP],
        v((2, 2, CH, D), BF16), v((2, 3, CH, FF), BF16),
        v((CHUNKS, 2, CH, HALF), BF16), v((CHUNKS, 3, CH, FF), BF16),
        v((D, CH), BF16),
        *[v((rows, w), BF16) for w in WR],
        *[v((4, TOK, w), BF16) for w in WR],
    ]
    dma = pltpu.SemaphoreType.DMA
    sems = [
        dma((4,)),
        *[dma((3,))] * 9,
        *[dma((3, 3))] * 4,
        *[dma((3,))] * 6,
    ]
    sums = v((1, HALF, FF), F32)
    token_grad, *grads = pl.pallas_call(
        body,
        out_shape=(v((TOK, D), BF16), sums, sums, sums),
        in_specs=[hbm] * 7,
        out_specs=(vm, vm, vm, vm),
        scratch_shapes=scratch + sems,
        compiler_params=pltpu.CompilerParams(
            collective_id=0, has_side_effects=True, vmem_limit_bytes=52500000
        ),
        name="routed_backward",
    )(expert_ids.T, combine.T, tokens, grad_out, w_gate, w_up, w_down)
    return (token_grad, *[g.astype(BF16) for g in grads])


def solution(mesh):
    rows = P(("dp", "expert"), None)
    weights = P("expert", "dp", None)
    return jax.shard_map(
        shards,
        mesh=mesh,
        in_specs=(rows, rows, rows, rows, weights, weights, weights),
        out_specs=(rows, weights, weights, weights),
        check_vma=False,
    )
```

```python
import jax
import jax.numpy as jnp
from jax import lax
from jax.experimental import pallas as pl
from jax.experimental.pallas import tpu as pltpu
from jax.sharding import PartitionSpec as P

MESH = pl.DeviceIdType.MESH
F32, BF16 = jnp.float32, jnp.bfloat16

TOK, TOP, D, FF = 64, 8, 1792, 1280
HALF = D // 2
CH = 256
CHUNKS = 3
TILES = FF // 256
IN_COLS = ((0, 640), (640, 1280), (1280, 1792))
GR_COLS = ((0, 512), (512, 1152), (1152, 1792))
RT_COLS = ((0, 640), (640, 1152), (1152, 1792))
WI = tuple(b - a for a, b in IN_COLS)
WG = tuple(b - a for a, b in GR_COLS)
WR = tuple(b - a for a, b in RT_COLS)
WP = tuple(a + b for a, b in zip(WI, WG))


def expert_of(p, line, j):
    if p == 0:
        return line * 16 + j
    if p == 1:
        return (j // 4) * 16 + line * 4 + j % 4
    return j * 4 + line


def dot(a, b):
    return jnp.dot(a, b, preferred_element_type=F32)


def dot_nt(a, b):
    return lax.dot_general(a, b, (((1,), (1,)), ((), ())), preferred_element_type=F32)


def dot_tn(a, b):
    return lax.dot_general(a, b, (((0,), (0,)), ((), ())), preferred_element_type=F32)


def body(
    ids_hbm, comb_hbm, tok_hbm, gout_hbm, wg_ref, wu_ref, wd_ref,
    tg_ref, og_ref, ou_ref, od_ref,
    ids_ref, comb_ref, tok_ref, gout_ref, wfull, line0, line1, line2, mytab, mytabs, tabs, r_tab, c_tab, w_rows, a_mat, perm,
    spk0, spk1, spk2, rx0, rx1, rx2, xg, hg, hgt, far_xg, far_hg, gx,
    rr0, rr1, rr2, lr0, lr1, lr2,
    i_loc, w_loc, w_send, w_recv, lt_send, lt_recv, x_send, x_recv, g_send, g_recv,
    d_send, d_recv, b_send, b_recv, l_send, l_recv, q_send, q_recv, h_send, h_recv, free_sem,
):
    lines, spk, rx = (line0, line1, line2), (spk0, spk1, spk2), (rx0, rx1, rx2)
    rr = (rr0, rr1, rr2)
    lr = (lr0, lr1, lr2)
    w_in = (wg_ref, wu_ref, wd_ref)
    w_out = (og_ref, ou_ref, od_ref)
    d = lax.axis_index("dp")
    e = lax.axis_index("expert")
    z, y, x = e // 16, (e // 4) % 4, e % 4
    lcoord = (z, y, x)
    jcoord = (y * 4 + x, z * 4 + x, z * 4 + y)
    partner = (1 - d, e)

    def peer_j(p, i):
        j = jcoord[p]
        return ((j // 4 + i // 4) % 4) * 4 + (j % 4 + i % 4) % 4

    def remote(src, dst, ss, rsem, device):
        return pltpu.make_async_remote_copy(
            src_ref=src, dst_ref=dst, send_sem=ss, recv_sem=rsem,
            device_id=device, device_id_type=MESH,
        )

    small = ((ids_hbm, ids_ref), (comb_hbm, comb_ref), (tok_hbm, tok_ref), (gout_hbm, gout_ref))
    for k, (src, dst) in enumerate(small):
        pltpu.make_async_copy(src, dst, i_loc.at[k]).start()

    barrier = pltpu.get_barrier_semaphore()

    def greet(p, i):
        pl.semaphore_signal(
            barrier, inc=1,
            device_id=(d, expert_of(p, lcoord[p], peer_j(p, i))), device_id_type=MESH,
        )

    for i in range(1, 16):
        greet(0, i)
        if i >= 4:
            greet(1, i)
            if i % 4:
                greet(2, i)
    pl.semaphore_signal(barrier, inc=1, device_id=partner, device_id_type=MESH)

    own_rows = pl.ds(pl.multiple_of(d * HALF, HALF), HALF)
    for w in range(3):
        pltpu.make_async_copy(w_in[w].at[0], wfull.at[w, own_rows], w_loc.at[w]).start()

    for k, (src, dst) in enumerate(small):
        pltpu.make_async_copy(src, dst, i_loc.at[k]).wait()
    ids = ids_ref[...].astype(F32)
    e_iota = lax.broadcasted_iota(jnp.int32, (64, TOK), 0).astype(F32)
    named = jnp.zeros((64, TOK), F32)
    for k in range(TOP):
        named = named + jnp.where(ids[k : k + 1, :] == e_iota, 1.0, 0.0)
    upper = (
        lax.broadcasted_iota(jnp.int32, (TOK, TOK), 0)
        < lax.broadcasted_iota(jnp.int32, (TOK, TOK), 1)
    )
    earlier = dot(named.astype(BF16), jnp.where(upper, 1.0, 0.0).astype(BF16))
    mytab[...] = jnp.zeros_like(mytab)
    mytab[0:8, 0:TOK] = ids
    for k in range(TOP):
        mytab[8 + k : 9 + k, 0:TOK] = jnp.sum(
            jnp.where(ids[k : k + 1, :] == e_iota, earlier, 0.0), axis=0, keepdims=True
        )
    mytab[16:24, 0:TOK] = comb_ref[...]
    low = mytab[...]
    high = pltpu.roll(low, 64, 1)
    for p in range(3):
        mytabs[p] = jnp.where(lcoord[p] % 2 == 0, low, high)

    pl.semaphore_wait(barrier, 37)

    for kind in range(3):
        for i in range(1, 4):
            for p in range(3):
                to = (d, expert_of(p, (lcoord[p] + i) % 4, jcoord[p]))
                rows = pl.ds(pl.multiple_of(lcoord[p] * TOK, TOK), TOK)
                if kind == 0:
                    remote(
                        mytabs.at[p], tabs.at[p, lcoord[p]], lt_send.at[p], lt_recv.at[p], to
                    ).start()
                elif kind == 1:
                    remote(
                        tok_ref.at[:, pl.ds(IN_COLS[p][0], WI[p])],
                        lines[p].at[rows, pl.ds(0, WI[p])],
                        x_send.at[p], x_recv.at[p], to,
                    ).start()
                else:
                    remote(
                        gout_ref.at[:, pl.ds(GR_COLS[p][0], WG[p])],
                        lines[p].at[rows, pl.ds(WI[p], WG[p])],
                        g_send.at[p], g_recv.at[p], to,
                    ).start()
    for w in range(3):
        remote(w_in[w].at[0], wfull.at[w, own_rows], w_send.at[w], w_recv.at[w], partner).start()

    for p in range(3):
        rows = pl.ds(pl.multiple_of(lcoord[p] * TOK, TOK), TOK)
        tabs[p, lcoord[p]] = mytabs[p]
        lines[p][rows, 0 : WI[p]] = tok_ref[:, IN_COLS[p][0] : IN_COLS[p][1]]
        lines[p][rows, WI[p] : WP[p]] = gout_ref[:, GR_COLS[p][0] : GR_COLS[p][1]]

    row0 = lax.broadcasted_iota(jnp.int32, (CH, CH), 0)
    col0 = lax.broadcasted_iota(jnp.int32, (CH, CH), 1)
    ry, rxx, rz, rk = (row0 >> 6) & 3, (row0 >> 4) & 3, (row0 >> 2) & 3, row0 & 3
    perm[0] = jnp.where(col0 == (rz << 6) + (rxx << 4) + (ry << 2) + rk, 1.0, 0.0).astype(BF16)
    perm[1] = jnp.where(col0 == (rz << 6) + (ry << 4) + (rxx << 2) + rk, 1.0, 0.0).astype(BF16)
    perm[2] = jnp.where(col0 == row0, 1.0, 0.0).astype(BF16)
    perm[3] = jnp.where(col0 == (rxx << 6) + (rz << 4) + (ry << 2) + rk, 1.0, 0.0).astype(BF16)

    for p in range(3):
        remote(tabs.at[p, pl.ds(0, 3)], tabs.at[p, pl.ds(0, 3)], lt_send.at[p], lt_recv.at[p], partner).wait_recv()
        table = jnp.concatenate([tabs[p, 0] + tabs[p, 1], tabs[p, 2] + tabs[p, 3]], axis=1)
        jj = lax.broadcasted_iota(jnp.int32, (16, 1), 0)
        if p == 0:
            code = jj + lcoord[0] * 16
        elif p == 1:
            code = ((jj >> 2) << 4) + (jj & 3) + lcoord[1] * 4
        else:
            code = (jj << 2) + lcoord[2]
        code = code.astype(F32)
        rank = jnp.zeros((16, CH), F32)
        weight = jnp.zeros((16, CH), F32)
        for k in range(TOP):
            here = table[k : k + 1, :] == code
            rank = rank + jnp.where(here, table[8 + k : 9 + k, :] + 1.0, 0.0)
            weight = weight + jnp.where(here, table[16 + k : 17 + k, :], 0.0)
        r_tab[p] = rank - 1.0
        c_tab[p] = weight

    def dispatch(c, start=(0, 0, 0), width=WP):
        crow = c * CH

        def send(i, carry2):
            for p in range(3):
                jj = peer_j(p, i)
                to = (d, expert_of(p, lcoord[p], jj))
                cols = pl.ds(start[p], width[p])
                remote(
                    spk[p].at[pl.ds(pl.multiple_of(crow + jj * 16, 16), 16), cols],
                    rx[p].at[pl.ds(pl.multiple_of(crow + jcoord[p] * 16, 16), 16), cols],
                    d_send.at[p, c], d_recv.at[p, c], to,
                ).start()
            return carry2

        lax.fori_loop(1, 16, send, 0)
        for p in range(3):
            mine = pl.ds(pl.multiple_of(crow + jcoord[p] * 16, 16), 16)
            cols = slice(start[p], start[p] + width[p])
            rx[p][mine, cols] = spk[p][mine, cols]

    def give_back(c, which=(0, 1, 2)):
        crow = c * CH

        def send(i, carry2):
            for p in which:
                jj = peer_j(p, i)
                to = (d, expert_of(p, lcoord[p], jj))
                remote(
                    spk[p].at[pl.ds(pl.multiple_of(crow + jj * 16, 16), 16), pl.ds(0, WR[p])],
                    rr[p].at[pl.ds(pl.multiple_of(crow + jcoord[p] * 16, 16), 16)],
                    b_send.at[p, c], b_recv.at[p, c], to,
                ).start()
            return carry2

        lax.fori_loop(1, 16, send, 0)
        for p in which:
            mine = pl.ds(pl.multiple_of(crow + jcoord[p] * 16, 16), 16)
            rr[p][mine, :] = spk[p][mine, 0 : WR[p]]

    def pack_rows(c):
        r_i = lax.broadcasted_iota(jnp.int32, (CH, CH), 0)
        s_i = lax.broadcasted_iota(jnp.int32, (CH, CH), 1) >> 6
        want = jnp.where(((r_i >> 2) & 3) == s_i, (r_i & 3) + 4 * c, -100).astype(F32)
        for p in range(3):
            rank = jnp.broadcast_to(r_tab[p][:, None, :], (16, 16, CH)).reshape(CH, CH)
            wt = jnp.broadcast_to(c_tab[p][:, None, :], (16, 16, CH)).reshape(CH, CH)
            hit = rank == want
            one = jnp.where(hit, 1.0, 0.0).astype(BF16)
            a_mat[p, c * CH : (c + 1) * CH, :] = one
            w_rows[p] = jnp.sum(jnp.where(hit, wt, 0.0), axis=1, keepdims=True)
            spk[p][c * CH : (c + 1) * CH, 0 : WI[p]] = dot(one, lines[p][:, 0 : WI[p]]).astype(BF16)

    def pack_grads(c):
        for p in range(3):
            one = a_mat[p, c * CH : (c + 1) * CH, :]
            spk[p][c * CH : (c + 1) * CH, WI[p] : WP[p]] = (
                dot(one, lines[p][:, WI[p] : WP[p]]) * w_rows[p]
            ).astype(BF16)

    for p in range(3):
        a = lines[p].at[pl.ds(0, 192), pl.ds(0, WI[p])]
        remote(a, a, x_send.at[p], x_recv.at[p], partner).wait_recv()
    pack_rows(0)
    dispatch(0, (0, 0, 0), WI)
    for p in range(3):
        b = lines[p].at[pl.ds(0, 192), pl.ds(WI[p], WG[p])]
        remote(b, b, g_send.at[p], g_recv.at[p], partner).wait_recv()
    pack_grads(0)
    dispatch(0, WI, WG)
    pack_rows(1)
    pack_grads(1)
    dispatch(1)
    pack_rows(2)
    pack_grads(2)

    def clear(n, carry):
        rows = pl.ds(pl.multiple_of(n * 128, 128), 128)
        for w in range(3):
            w_out[w][0, rows, :] = jnp.zeros((128, FF), F32)
        return carry

    lax.fori_loop(0, HALF // 128, clear, 0)

    for w in range(3):
        pltpu.make_async_copy(w_in[w].at[0], wfull.at[w, own_rows], w_loc.at[w]).wait()
        remote(w_in[w].at[0], wfull.at[w, own_rows], w_send.at[w], w_recv.at[w], partner).wait()

    near = pl.ds(pl.multiple_of(d * HALF, 128), HALF)
    far = pl.ds(pl.multiple_of((1 - d) * HALF, 128), HALF)

    def far_wait(c):
        remote(far_xg.at[c % 2], far_xg.at[c % 2], q_send.at[c], q_recv.at[c], partner).wait_recv()
        remote(far_hg.at[c % 2], far_hg.at[c % 2], h_send.at[c], h_recv.at[c], partner).wait_recv()

    def terms(c, n):
        b = c % 2
        cols = slice(n * 256, n * 256 + 256)
        for w in range(3):
            k = w // 2
            w_out[w][0, :, cols] += dot_tn(xg[b, k, :, near], hg[b, w, :, cols]) + dot_tn(
                far_xg[b, k], far_hg[b, w, :, cols]
            )

    def compute(c, carry):
        crow = pl.multiple_of(c * CH, CH)
        rows = pl.ds(crow, CH)
        b = c % 2

        @pl.when(c >= 2)
        def _():
            remote(far_xg.at[0], far_xg.at[0], q_send.at[0], q_recv.at[0], partner).wait_send()
            remote(far_hg.at[0], far_hg.at[0], h_send.at[0], h_recv.at[0], partner).wait_send()
            pl.semaphore_wait(free_sem, 1)

        for p in range(3):
            part = rx[p].at[pl.ds(0, 240)]
            remote(part, part, d_send.at[p, c], d_recv.at[p, c], partner).wait_recv()

        @pl.when(c >= 1)
        def _():
            give_back(c - 1)

        for p in range(3):
            i0, i1 = IN_COLS[p]
            g0, g1 = GR_COLS[p]
            if p == 0:
                xg[b, 0, :, i0:i1] = rx[0][rows, 0 : WI[0]]
                xg[b, 1, :, g0:g1] = rx[0][rows, WI[0] : WP[0]]
            else:
                xg[b, 0, :, i0:i1] = dot(perm[p - 1], rx[p][rows, 0 : WI[p]]).astype(BF16)
                xg[b, 1, :, g0:g1] = dot(perm[p - 1], rx[p][rows, WI[p] : WP[p]]).astype(BF16)
        for k in range(2):
            remote(
                xg.at[b, k, :, far], far_xg.at[b, k], q_send.at[c], q_recv.at[c], partner
            ).start()

        def units(n):
            cols = slice(n * 256, n * 256 + 256)
            gate = dot(xg[b, 0], wfull[0, :, cols])
            up = dot(xg[b, 0], wfull[1, :, cols])
            gh = dot(xg[b, 1], wfull[2, :, cols])
            sig = jax.nn.sigmoid(gate)
            act = gate * sig
            hg[b, 2, :, cols] = (act * up).astype(BF16)
            grad_gate = (gh * up * sig * (1.0 + gate * (1.0 - sig))).astype(BF16)
            grad_up = (gh * act).astype(BF16)
            hg[b, 0, :, cols] = grad_gate
            hg[b, 1, :, cols] = grad_up
            hgt[0, cols, :] = grad_gate.T
            hgt[1, cols, :] = grad_up.T

        for n in range(TILES):
            units(n)

        @pl.when(c == 0)
        def _():
            dispatch(2)

        for k in range(3):
            remote(hg.at[b, k], far_hg.at[b, k], h_send.at[c], h_recv.at[c], partner).start()

        for p in range(3):
            part = rx[p].at[pl.ds(0, 240)]
            remote(part, part, d_send.at[p, c], d_recv.at[p, c], partner).wait_send()
            for n in ((0, 1, 2), (3, 4), (5, 6))[p]:
                tile = slice(n * 256, n * 256 + 256)
                gx[tile, :] = (
                    dot(wfull[0, tile, :], hgt[0]) + dot(wfull[1, tile, :], hgt[1])
                ).astype(BF16)
            third = slice(*RT_COLS[p])
            back = perm[(2, 0, 3)[p]]
            spk[p][rows, 0 : WR[p]] = dot_nt(back, gx[third, :]).astype(BF16)

            @pl.when(c == CHUNKS - 1)
            def _():
                give_back(CHUNKS - 1, (p,))

        @pl.when(c == 0)
        def _():
            far_wait(c)
            for n in range(TILES):
                terms(0, n)
            pl.semaphore_signal(free_sem, inc=1, device_id=partner, device_id_type=MESH)

        return carry

    lax.fori_loop(0, CHUNKS, compute, 0)
    far_wait(1)
    far_wait(2)

    def late_terms(start, stop):
        for i in range(start, stop):
            terms(1 + i // TILES, i % TILES)

    late_terms(0, TILES + 1)

    for p in range(3):
        for c in range(CHUNKS):
            part = rr[p].at[pl.ds(0, 240)]
            remote(part, part, b_send.at[p, c], b_recv.at[p, c], partner).wait_recv()
        lines[p][:, 0 : WR[p]] = dot_tn(a_mat[p], rr[p][...]).astype(BF16)
        for i in range(1, 4):
            s = (lcoord[p] + i) % 4
            to = (d, expert_of(p, s, jcoord[p]))
            remote(
                lines[p].at[pl.ds(pl.multiple_of(s * TOK, TOK), TOK), pl.ds(0, WR[p])],
                lr[p].at[lcoord[p]],
                l_send.at[p], l_recv.at[p], to,
            ).start()
        lr[p][lcoord[p]] = lines[p][
            pl.ds(pl.multiple_of(lcoord[p] * TOK, TOK), TOK), 0 : WR[p]
        ]

    late_terms(TILES + 1, 2 * TILES)

    for p in range(3):
        part = lr[p].at[pl.ds(0, 3)]
        remote(part, part, l_send.at[p], l_recv.at[p], partner).wait_recv()
        total = lr[p][0].astype(F32) + lr[p][1].astype(F32)
        total = total + lr[p][2].astype(F32) + lr[p][3].astype(F32)
        tg_ref[:, RT_COLS[p][0] : RT_COLS[p][1]] = total.astype(BF16)

    for p in range(3):
        remote(tabs.at[p, pl.ds(0, 3)], tabs.at[p, pl.ds(0, 3)], lt_send.at[p], lt_recv.at[p], partner).wait_send()
        a = lines[p].at[pl.ds(0, 192), pl.ds(0, WI[p])]
        b = lines[p].at[pl.ds(0, 192), pl.ds(WI[p], WG[p])]
        remote(a, a, x_send.at[p], x_recv.at[p], partner).wait_send()
        remote(b, b, g_send.at[p], g_recv.at[p], partner).wait_send()
        for c in range(CHUNKS):
            part = rr[p].at[pl.ds(0, 240)]
            remote(part, part, b_send.at[p, c], b_recv.at[p, c], partner).wait_send()
        part = lr[p].at[pl.ds(0, 3)]
        remote(part, part, l_send.at[p], l_recv.at[p], partner).wait_send()
    for c in range(1, CHUNKS):
        remote(far_xg.at[c % 2], far_xg.at[c % 2], q_send.at[c], q_recv.at[c], partner).wait_send()
        remote(far_hg.at[c % 2], far_hg.at[c % 2], h_send.at[c], h_recv.at[c], partner).wait_send()


def finish(tg_ref, sg_ref, su_ref, sd_ref, tg_out, g_out, u_out, d_out, g_b, u_b, d_b, t_sem, sem):
    token = pltpu.make_async_copy(tg_ref, tg_out, t_sem)
    token.start()
    groups = ((sg_ref, g_b, g_out), (su_ref, u_b, u_out), (sd_ref, d_b, d_out))

    def tile(n, carry):
        rows = pl.ds(pl.multiple_of(n * 128, 128), 128)
        for w, (total, held, out) in enumerate(groups):
            held[rows, :] = total[0, rows, :].astype(BF16)
            pltpu.make_async_copy(held.at[rows], out.at[0, rows], sem.at[w]).start()
        return carry

    lax.fori_loop(0, HALF // 128, tile, 0)
    for w, (_, held, out) in enumerate(groups):
        pltpu.make_async_copy(held, out.at[0], sem.at[w]).wait()
    token.wait()


def shards(tokens, grad_out, combine, expert_ids, w_gate, w_up, w_down):
    vm, hbm = pl.BlockSpec(memory_space=pltpu.VMEM), pl.BlockSpec(memory_space=pl.ANY)
    rows = CHUNKS * CH
    v = pltpu.VMEM
    scratch = [
        v((TOP, TOK), jnp.int32), v((TOP, TOK), F32), v((TOK, D), BF16), v((TOK, D), BF16),
        v((3, D, FF), BF16),
        *[v((CH, w), BF16) for w in WP],
        v((24, 128), F32), v((3, 24, 128), F32), v((3, 4, 24, 128), F32),
        v((3, 16, CH), F32), v((3, 16, CH), F32), v((3, CH, 1), F32),
        v((3, rows, CH), BF16), v((4, CH, CH), BF16),
        *[v((rows, w), BF16) for w in WP],
        *[v((rows, w), BF16) for w in WP],
        v((2, 2, CH, D), BF16), v((2, 3, CH, FF), BF16), v((2, FF, CH), BF16),
        v((2, 2, CH, HALF), BF16), v((2, 3, CH, FF), BF16),
        v((D, CH), BF16),
        *[v((rows, w), BF16) for w in WR],
        *[v((4, TOK, w), BF16) for w in WR],
    ]
    dma = pltpu.SemaphoreType.DMA
    sems = [
        dma((4,)),
        *[dma((3,))] * 9,
        *[dma((3, 3))] * 4,
        *[dma((3,))] * 6,
        pltpu.SemaphoreType.REGULAR,
    ]
    sums = v((1, HALF, FF), F32)
    token_grad, *grads = pl.pallas_call(
        body,
        out_shape=(v((TOK, D), BF16), sums, sums, sums),
        in_specs=[hbm] * 7,
        out_specs=(vm, vm, vm, vm),
        scratch_shapes=scratch + sems,
        compiler_params=pltpu.CompilerParams(
            collective_id=0, has_side_effects=True, vmem_limit_bytes=52900000
        ),
        name="routed_backward",
    )(expert_ids.T, combine.T, tokens, grad_out, w_gate, w_up, w_down)
    hold = [v((HALF, FF), BF16)] * 3
    return pl.pallas_call(
        finish,
        out_shape=[jax.ShapeDtypeStruct((TOK, D), BF16)]
        + [jax.ShapeDtypeStruct((1, HALF, FF), BF16)] * 3,
        in_specs=[vm] * 4,
        out_specs=[hbm] * 4,
        scratch_shapes=hold + [dma, dma((3,))],
        compiler_params=pltpu.CompilerParams(vmem_limit_bytes=16 << 20),
        name="finish",
    )(token_grad, *grads)


def solution(mesh):
    rows = P(("dp", "expert"), None)
    weights = P("expert", "dp", None)
    return jax.shard_map(
        shards,
        mesh=mesh,
        in_specs=(rows, rows, rows, rows, weights, weights, weights),
        out_specs=(rows, weights, weights, weights),
        check_vma=False,
    )
```

```python
import jax
import jax.numpy as jnp
from jax import lax
from jax.experimental import pallas as pl
from jax.experimental.pallas import tpu as pltpu
from jax.sharding import PartitionSpec as P

MESH = pl.DeviceIdType.MESH
F32, BF16 = jnp.float32, jnp.bfloat16

TOK, TOP, D, FF = 64, 8, 1792, 1280
HALF = D // 2
CH = 256
CHUNKS = 3
TILES = FF // 256
IN_COLS = ((0, 640), (640, 1280), (1280, 1792))
GR_COLS = ((0, 512), (512, 1152), (1152, 1792))
RT_COLS = ((0, 640), (640, 1152), (1152, 1792))
WI = tuple(b - a for a, b in IN_COLS)
WG = tuple(b - a for a, b in GR_COLS)
WR = tuple(b - a for a, b in RT_COLS)
WP = tuple(a + b for a, b in zip(WI, WG))


def expert_of(p, line, j):
    if p == 0:
        return line * 16 + j
    if p == 1:
        return (j // 4) * 16 + line * 4 + j % 4
    return j * 4 + line


def dot(a, b):
    return jnp.dot(a, b, preferred_element_type=F32)


def dot_nt(a, b):
    return lax.dot_general(a, b, (((1,), (1,)), ((), ())), preferred_element_type=F32)


def dot_tn(a, b):
    return lax.dot_general(a, b, (((0,), (0,)), ((), ())), preferred_element_type=F32)


def body(
    ids_hbm, comb_hbm, tok_hbm, gout_hbm, wg_ref, wu_ref, wd_ref,
    tg_ref, og_ref, ou_ref, od_ref,
    ids_ref, comb_ref, tok_ref, gout_ref, wfull, line0, line1, line2, mytab, mytabs, tabs, r_tab, c_tab, a_mat, perm,
    spk0, spk1, spk2, rx0, rx1, rx2, xg, hg, hgt, far_xg, far_hg, gx,
    rr0, rr1, rr2, lr0, lr1, lr2,
    i_loc, w_loc, w_send, w_recv, lt_send, lt_recv, x_send, x_recv, g_send, g_recv,
    d_send, d_recv, b_send, b_recv, l_send, l_recv, q_send, q_recv, h_send, h_recv, free_sem,
):
    lines, spk, rx = (line0, line1, line2), (spk0, spk1, spk2), (rx0, rx1, rx2)
    rr = (rr0, rr1, rr2)
    lr = (lr0, lr1, lr2)
    w_in = (wg_ref, wu_ref, wd_ref)
    w_out = (og_ref, ou_ref, od_ref)
    d = lax.axis_index("dp")
    e = lax.axis_index("expert")
    z, y, x = e // 16, (e // 4) % 4, e % 4
    lcoord = (z, y, x)
    jcoord = (y * 4 + x, z * 4 + x, z * 4 + y)
    partner = (1 - d, e)

    def peer_j(p, i):
        j = jcoord[p]
        if p == 1:
            return ((j // 4 + i % 4) % 4) * 4 + (j % 4 + i // 4) % 4
        return ((j // 4 + i // 4) % 4) * 4 + (j % 4 + i % 4) % 4

    def remote(src, dst, ss, rsem, device):
        return pltpu.make_async_remote_copy(
            src_ref=src, dst_ref=dst, send_sem=ss, recv_sem=rsem,
            device_id=device, device_id_type=MESH,
        )

    small = ((ids_hbm, ids_ref), (comb_hbm, comb_ref), (tok_hbm, tok_ref), (gout_hbm, gout_ref))
    for k, (src, dst) in enumerate(small):
        pltpu.make_async_copy(src, dst, i_loc.at[k]).start()

    barrier = pltpu.get_barrier_semaphore()

    def greet(p, i):
        pl.semaphore_signal(
            barrier, inc=1,
            device_id=(d, expert_of(p, lcoord[p], peer_j(p, i))), device_id_type=MESH,
        )

    for i in range(1, 16):
        greet(0, i)
        if i % 4:
            greet(1, i)
            if i >= 4:
                greet(2, i)
    pl.semaphore_signal(barrier, inc=1, device_id=partner, device_id_type=MESH)

    own_rows = pl.ds(pl.multiple_of(d * HALF, HALF), HALF)
    for w in range(3):
        pltpu.make_async_copy(w_in[w].at[0], wfull.at[w, own_rows], w_loc.at[w]).start()

    for k, (src, dst) in enumerate(small):
        pltpu.make_async_copy(src, dst, i_loc.at[k]).wait()
    ids = ids_ref[...].astype(F32)
    e_iota = lax.broadcasted_iota(jnp.int32, (64, TOK), 0).astype(F32)
    named = jnp.zeros((64, TOK), F32)
    for k in range(TOP):
        named = named + jnp.where(ids[k : k + 1, :] == e_iota, 1.0, 0.0)
    upper = (
        lax.broadcasted_iota(jnp.int32, (TOK, TOK), 0)
        < lax.broadcasted_iota(jnp.int32, (TOK, TOK), 1)
    )
    earlier = dot(named.astype(BF16), jnp.where(upper, 1.0, 0.0).astype(BF16))
    mytab[...] = jnp.zeros_like(mytab)
    mytab[0:8, 0:TOK] = ids
    for k in range(TOP):
        mytab[8 + k : 9 + k, 0:TOK] = jnp.sum(
            jnp.where(ids[k : k + 1, :] == e_iota, earlier, 0.0), axis=0, keepdims=True
        )
    mytab[16:24, 0:TOK] = comb_ref[...]
    low = mytab[...]
    high = pltpu.roll(low, 64, 1)
    for p in range(3):
        mytabs[p] = jnp.where(lcoord[p] % 2 == 0, low, high)

    pl.semaphore_wait(barrier, 37)

    for kind in range(3):
        for i in range(1, 4):
            for p in range(3):
                to = (d, expert_of(p, (lcoord[p] + i) % 4, jcoord[p]))
                rows = pl.ds(pl.multiple_of(lcoord[p] * TOK, TOK), TOK)
                if kind == 0:
                    remote(
                        mytabs.at[p], tabs.at[p, lcoord[p]], lt_send.at[p], lt_recv.at[p], to
                    ).start()
                elif kind == 1:
                    remote(
                        tok_ref.at[:, pl.ds(IN_COLS[p][0], WI[p])],
                        lines[p].at[rows, pl.ds(0, WI[p])],
                        x_send.at[p], x_recv.at[p], to,
                    ).start()
                else:
                    remote(
                        gout_ref.at[:, pl.ds(GR_COLS[p][0], WG[p])],
                        lines[p].at[rows, pl.ds(WI[p], WG[p])],
                        g_send.at[p], g_recv.at[p], to,
                    ).start()
    for w in range(3):
        remote(w_in[w].at[0], wfull.at[w, own_rows], w_send.at[w], w_recv.at[w], partner).start()

    for p in range(3):
        rows = pl.ds(pl.multiple_of(lcoord[p] * TOK, TOK), TOK)
        tabs[p, lcoord[p]] = mytabs[p]
        lines[p][rows, 0 : WI[p]] = tok_ref[:, IN_COLS[p][0] : IN_COLS[p][1]]
        lines[p][rows, WI[p] : WP[p]] = gout_ref[:, GR_COLS[p][0] : GR_COLS[p][1]]

    row0 = lax.broadcasted_iota(jnp.int32, (CH, CH), 0)
    col0 = lax.broadcasted_iota(jnp.int32, (CH, CH), 1)
    ry, rxx, rz, rk = (row0 >> 6) & 3, (row0 >> 4) & 3, (row0 >> 2) & 3, row0 & 3
    perm[0] = jnp.where(col0 == (rz << 6) + (rxx << 4) + (ry << 2) + rk, 1.0, 0.0).astype(BF16)
    perm[1] = jnp.where(col0 == (rz << 6) + (ry << 4) + (rxx << 2) + rk, 1.0, 0.0).astype(BF16)
    perm[2] = jnp.where(col0 == row0, 1.0, 0.0).astype(BF16)
    perm[3] = jnp.where(col0 == (rxx << 6) + (rz << 4) + (ry << 2) + rk, 1.0, 0.0).astype(BF16)

    for p in range(3):
        remote(tabs.at[p, pl.ds(0, 3)], tabs.at[p, pl.ds(0, 3)], lt_send.at[p], lt_recv.at[p], partner).wait_recv()
        table = jnp.concatenate([tabs[p, 0] + tabs[p, 1], tabs[p, 2] + tabs[p, 3]], axis=1)
        jj = lax.broadcasted_iota(jnp.int32, (16, 1), 0)
        if p == 0:
            code = jj + lcoord[0] * 16
        elif p == 1:
            code = ((jj >> 2) << 4) + (jj & 3) + lcoord[1] * 4
        else:
            code = (jj << 2) + lcoord[2]
        code = code.astype(F32)
        rank = jnp.zeros((16, CH), F32)
        weight = jnp.zeros((16, CH), F32)
        for k in range(TOP):
            here = table[k : k + 1, :] == code
            rank = rank + jnp.where(here, table[8 + k : 9 + k, :] + 1.0, 0.0)
            weight = weight + jnp.where(here, table[16 + k : 17 + k, :], 0.0)
        r_tab[p] = rank - 1.0
        c_tab[p] = weight

    def dispatch(c, start=(0, 0, 0), width=WP):
        crow = c * CH

        def send(i, carry2):
            for p in range(3):
                jj = peer_j(p, i)
                to = (d, expert_of(p, lcoord[p], jj))
                cols = pl.ds(start[p], width[p])
                remote(
                    spk[p].at[pl.ds(pl.multiple_of(crow + jj * 16, 16), 16), cols],
                    rx[p].at[pl.ds(pl.multiple_of(crow + jcoord[p] * 16, 16), 16), cols],
                    d_send.at[p, c], d_recv.at[p, c], to,
                ).start()
            return carry2

        lax.fori_loop(1, 16, send, 0)
        for p in range(3):
            mine = pl.ds(pl.multiple_of(crow + jcoord[p] * 16, 16), 16)
            cols = slice(start[p], start[p] + width[p])
            rx[p][mine, cols] = spk[p][mine, cols]

    def give_back(c, which=(0, 1, 2)):
        crow = c * CH

        def send(i, carry2):
            for p in which:
                jj = peer_j(p, i)
                to = (d, expert_of(p, lcoord[p], jj))
                remote(
                    spk[p].at[pl.ds(pl.multiple_of(crow + jj * 16, 16), 16), pl.ds(0, WR[p])],
                    rr[p].at[pl.ds(pl.multiple_of(crow + jcoord[p] * 16, 16), 16)],
                    b_send.at[p, c], b_recv.at[p, c], to,
                ).start()
            return carry2

        lax.fori_loop(1, 16, send, 0)
        for p in which:
            mine = pl.ds(pl.multiple_of(crow + jcoord[p] * 16, 16), 16)
            rr[p][mine, :] = spk[p][mine, 0 : WR[p]]

    def pack_rows(c):
        r_i = lax.broadcasted_iota(jnp.int32, (CH, CH), 0)
        s_i = lax.broadcasted_iota(jnp.int32, (CH, CH), 1) >> 6
        want = jnp.where(((r_i >> 2) & 3) == s_i, (r_i & 3) + 4 * c, -100).astype(F32)
        for p in range(3):
            rank = jnp.broadcast_to(r_tab[p][:, None, :], (16, 16, CH)).reshape(CH, CH)
            one = jnp.where(rank == want, 1.0, 0.0).astype(BF16)
            a_mat[p, c * CH : (c + 1) * CH, :] = one
            spk[p][c * CH : (c + 1) * CH, 0 : WI[p]] = dot(one, lines[p][:, 0 : WI[p]]).astype(BF16)

    def pack_grads(c):
        for p in range(3):
            one = a_mat[p, c * CH : (c + 1) * CH, :]
            wt = jnp.broadcast_to(c_tab[p][:, None, :], (16, 16, CH)).reshape(CH, CH)
            w_row = jnp.sum(one.astype(F32) * wt, axis=1, keepdims=True)
            spk[p][c * CH : (c + 1) * CH, WI[p] : WP[p]] = (
                dot(one, lines[p][:, WI[p] : WP[p]]) * w_row
            ).astype(BF16)

    for p in range(3):
        a = lines[p].at[pl.ds(0, 192), pl.ds(0, WI[p])]
        remote(a, a, x_send.at[p], x_recv.at[p], partner).wait_recv()
    pack_rows(0)
    dispatch(0, (0, 0, 0), WI)
    for p in range(3):
        b = lines[p].at[pl.ds(0, 192), pl.ds(WI[p], WG[p])]
        remote(b, b, g_send.at[p], g_recv.at[p], partner).wait_recv()
    pack_grads(0)
    dispatch(0, WI, WG)
    pack_rows(1)
    pack_grads(1)
    dispatch(1)
    pack_rows(2)
    pack_grads(2)

    def clear(n, carry):
        rows = pl.ds(pl.multiple_of(n * 128, 128), 128)
        for w in range(3):
            w_out[w][0, rows, :] = jnp.zeros((128, FF), F32)
        return carry

    lax.fori_loop(0, HALF // 128, clear, 0)

    for w in range(3):
        pltpu.make_async_copy(w_in[w].at[0], wfull.at[w, own_rows], w_loc.at[w]).wait()
        remote(w_in[w].at[0], wfull.at[w, own_rows], w_send.at[w], w_recv.at[w], partner).wait()

    near = pl.ds(pl.multiple_of(d * HALF, 128), HALF)
    far = pl.ds(pl.multiple_of((1 - d) * HALF, 128), HALF)

    def far_wait(c):
        remote(far_xg.at[c % 2], far_xg.at[c % 2], q_send.at[c], q_recv.at[c], partner).wait_recv()
        remote(far_hg.at[c % 2], far_hg.at[c % 2], h_send.at[c], h_recv.at[c], partner).wait_recv()

    def terms(c, n):
        b = c % 2
        cols = slice(n * 256, n * 256 + 256)
        for w in range(3):
            k = w // 2
            w_out[w][0, :, cols] += dot_tn(xg[b, k, :, near], hg[b, w, :, cols]) + dot_tn(
                far_xg[b, k], far_hg[b, w, :, cols]
            )

    def compute(c, carry):
        crow = pl.multiple_of(c * CH, CH)
        rows = pl.ds(crow, CH)
        b = c % 2

        @pl.when(c >= 2)
        def _():
            remote(far_xg.at[0], far_xg.at[0], q_send.at[0], q_recv.at[0], partner).wait_send()
            remote(far_hg.at[0], far_hg.at[0], h_send.at[0], h_recv.at[0], partner).wait_send()
            pl.semaphore_wait(free_sem, 1)

        for p in range(3):
            part = rx[p].at[pl.ds(0, 240)]
            remote(part, part, d_send.at[p, c], d_recv.at[p, c], partner).wait_recv()

        for p in range(3):
            i0, i1 = IN_COLS[p]
            g0, g1 = GR_COLS[p]
            if p == 0:
                xg[b, 0, :, i0:i1] = rx[0][rows, 0 : WI[0]]
                xg[b, 1, :, g0:g1] = rx[0][rows, WI[0] : WP[0]]
            else:
                xg[b, 0, :, i0:i1] = dot(perm[p - 1], rx[p][rows, 0 : WI[p]]).astype(BF16)
                xg[b, 1, :, g0:g1] = dot(perm[p - 1], rx[p][rows, WI[p] : WP[p]]).astype(BF16)
        for k in range(2):
            remote(
                xg.at[b, k, :, far], far_xg.at[b, k], q_send.at[c], q_recv.at[c], partner
            ).start()

        def units(n):
            cols = slice(n * 256, n * 256 + 256)
            gate = dot(xg[b, 0], wfull[0, :, cols])
            up = dot(xg[b, 0], wfull[1, :, cols])
            gh = dot(xg[b, 1], wfull[2, :, cols])
            sig = jax.nn.sigmoid(gate)
            act = gate * sig
            hg[b, 2, :, cols] = (act * up).astype(BF16)
            grad_gate = (gh * up * sig * (1.0 + gate * (1.0 - sig))).astype(BF16)
            grad_up = (gh * act).astype(BF16)
            hg[b, 0, :, cols] = grad_gate
            hg[b, 1, :, cols] = grad_up
            hgt[0, cols, :] = grad_gate.T
            hgt[1, cols, :] = grad_up.T

        for n in range(TILES):
            units(n)

        @pl.when(c == 0)
        def _():
            dispatch(2)

        @pl.when(c == 1)
        def _():
            give_back(0)

        for k in range(3):
            remote(hg.at[b, k], far_hg.at[b, k], h_send.at[c], h_recv.at[c], partner).start()

        for p in range(3):
            part = rx[p].at[pl.ds(0, 240)]
            remote(part, part, d_send.at[p, c], d_recv.at[p, c], partner).wait_send()
            for n in ((0, 1, 2), (3, 4), (5, 6))[p]:
                tile = slice(n * 256, n * 256 + 256)
                gx[tile, :] = (
                    dot(wfull[0, tile, :], hgt[0]) + dot(wfull[1, tile, :], hgt[1])
                ).astype(BF16)
            third = slice(*RT_COLS[p])
            back = perm[(2, 0, 3)[p]]
            spk[p][rows, 0 : WR[p]] = dot_nt(back, gx[third, :]).astype(BF16)

            @pl.when(c == CHUNKS - 1)
            def _():
                give_back(CHUNKS - 1, (p,))

        @pl.when(c == 1)
        def _():
            give_back(1)

        @pl.when(c == 0)
        def _():
            far_wait(c)
            for n in range(TILES):
                terms(0, n)
            pl.semaphore_signal(free_sem, inc=1, device_id=partner, device_id_type=MESH)

        return carry

    lax.fori_loop(0, CHUNKS, compute, 0)
    far_wait(1)
    far_wait(2)

    def late_terms(start, stop):
        for i in range(start, stop):
            terms(1 + i // TILES, i % TILES)

    late_terms(0, TILES + 1)

    for p in range(3):
        for c in range(CHUNKS):
            part = rr[p].at[pl.ds(0, 240)]
            remote(part, part, b_send.at[p, c], b_recv.at[p, c], partner).wait_recv()
        lines[p][:, 0 : WR[p]] = dot_tn(a_mat[p], rr[p][...]).astype(BF16)
        for i in range(1, 4):
            s = (lcoord[p] + i) % 4
            to = (d, expert_of(p, s, jcoord[p]))
            remote(
                lines[p].at[pl.ds(pl.multiple_of(s * TOK, TOK), TOK), pl.ds(0, WR[p])],
                lr[p].at[lcoord[p]],
                l_send.at[p], l_recv.at[p], to,
            ).start()
        lr[p][lcoord[p]] = lines[p][
            pl.ds(pl.multiple_of(lcoord[p] * TOK, TOK), TOK), 0 : WR[p]
        ]

    late_terms(TILES + 1, 2 * TILES)

    for p in range(3):
        part = lr[p].at[pl.ds(0, 3)]
        remote(part, part, l_send.at[p], l_recv.at[p], partner).wait_recv()
        total = lr[p][0].astype(F32) + lr[p][1].astype(F32)
        total = total + lr[p][2].astype(F32) + lr[p][3].astype(F32)
        tg_ref[:, RT_COLS[p][0] : RT_COLS[p][1]] = total.astype(BF16)

    for p in range(3):
        remote(tabs.at[p, pl.ds(0, 3)], tabs.at[p, pl.ds(0, 3)], lt_send.at[p], lt_recv.at[p], partner).wait_send()
        a = lines[p].at[pl.ds(0, 192), pl.ds(0, WI[p])]
        b = lines[p].at[pl.ds(0, 192), pl.ds(WI[p], WG[p])]
        remote(a, a, x_send.at[p], x_recv.at[p], partner).wait_send()
        remote(b, b, g_send.at[p], g_recv.at[p], partner).wait_send()
        for c in range(CHUNKS):
            part = rr[p].at[pl.ds(0, 240)]
            remote(part, part, b_send.at[p, c], b_recv.at[p, c], partner).wait_send()
        part = lr[p].at[pl.ds(0, 3)]
        remote(part, part, l_send.at[p], l_recv.at[p], partner).wait_send()
    for c in range(1, CHUNKS):
        remote(far_xg.at[c % 2], far_xg.at[c % 2], q_send.at[c], q_recv.at[c], partner).wait_send()
        remote(far_hg.at[c % 2], far_hg.at[c % 2], h_send.at[c], h_recv.at[c], partner).wait_send()


def finish(tg_ref, sg_ref, su_ref, sd_ref, tg_out, g_out, u_out, d_out, g_b, u_b, d_b, t_sem, sem):
    token = pltpu.make_async_copy(tg_ref, tg_out, t_sem)
    token.start()
    groups = ((sg_ref, g_b, g_out), (su_ref, u_b, u_out), (sd_ref, d_b, d_out))

    def tile(n, carry):
        rows = pl.ds(pl.multiple_of(n * 128, 128), 128)
        for w, (total, held, out) in enumerate(groups):
            held[rows, :] = total[0, rows, :].astype(BF16)
            pltpu.make_async_copy(held.at[rows], out.at[0, rows], sem.at[w]).start()
        return carry

    lax.fori_loop(0, HALF // 128, tile, 0)
    for w, (_, held, out) in enumerate(groups):
        pltpu.make_async_copy(held, out.at[0], sem.at[w]).wait()
    token.wait()


def shards(tokens, grad_out, combine, expert_ids, w_gate, w_up, w_down):
    vm, hbm = pl.BlockSpec(memory_space=pltpu.VMEM), pl.BlockSpec(memory_space=pl.ANY)
    rows = CHUNKS * CH
    v = pltpu.VMEM
    scratch = [
        v((TOP, TOK), jnp.int32), v((TOP, TOK), F32), v((TOK, D), BF16), v((TOK, D), BF16),
        v((3, D, FF), BF16),
        *[v((CH, w), BF16) for w in WP],
        v((24, 128), F32), v((3, 24, 128), F32), v((3, 4, 24, 128), F32),
        v((3, 16, CH), F32), v((3, 16, CH), F32),
        v((3, rows, CH), BF16), v((4, CH, CH), BF16),
        *[v((rows, w), BF16) for w in WP],
        *[v((rows, w), BF16) for w in WP],
        v((2, 2, CH, D), BF16), v((2, 3, CH, FF), BF16), v((2, FF, CH), BF16),
        v((2, 2, CH, HALF), BF16), v((2, 3, CH, FF), BF16),
        v((D, CH), BF16),
        *[v((rows, w), BF16) for w in WR],
        *[v((4, TOK, w), BF16) for w in WR],
    ]
    dma = pltpu.SemaphoreType.DMA
    sems = [
        dma((4,)),
        *[dma((3,))] * 9,
        *[dma((3, 3))] * 4,
        *[dma((3,))] * 6,
        pltpu.SemaphoreType.REGULAR,
    ]
    sums = v((1, HALF, FF), F32)
    token_grad, *grads = pl.pallas_call(
        body,
        out_shape=(v((TOK, D), BF16), sums, sums, sums),
        in_specs=[hbm] * 7,
        out_specs=(vm, vm, vm, vm),
        scratch_shapes=scratch + sems,
        compiler_params=pltpu.CompilerParams(
            collective_id=0, has_side_effects=True, vmem_limit_bytes=52900000
        ),
        name="routed_backward",
    )(expert_ids.T, combine.T, tokens, grad_out, w_gate, w_up, w_down)
    hold = [v((HALF, FF), BF16)] * 3
    return pl.pallas_call(
        finish,
        out_shape=[jax.ShapeDtypeStruct((TOK, D), BF16)]
        + [jax.ShapeDtypeStruct((1, HALF, FF), BF16)] * 3,
        in_specs=[vm] * 4,
        out_specs=[hbm] * 4,
        scratch_shapes=hold + [dma, dma((3,))],
        compiler_params=pltpu.CompilerParams(vmem_limit_bytes=16 << 20),
        name="finish",
    )(token_grad, *grads)


def solution(mesh):
    rows = P(("dp", "expert"), None)
    weights = P("expert", "dp", None)
    return jax.shard_map(
        shards,
        mesh=mesh,
        in_specs=(rows, rows, rows, rows, weights, weights, weights),
        out_specs=(rows, weights, weights, weights),
        check_vma=False,
    )
```
